128 devices in a mesh: bx: 32 (over y, x_lo, z), by: 4 (over x_hi, core).
Axes of the slice: x: 4 (x_hi: 2, x_lo: 2; x = x_hi * 2 + x_lo), y: 4, z: 4, core: 2. Of those that a mesh axis runs over, the one named last changes fastest.
Arguments:
- displacement: float32 [3, 64, 512, 256], P(None, 'bx', 'by'), may hold values from -0.06 to 0.06
- velocity: float32 [3, 64, 512, 256], P(None, 'bx', 'by'), may hold values from -1.5 to 1.5
- zone_mass: float32 [64, 512, 256], P('bx', 'by'), may hold values from 0.8 to 1.25
- energy: float32 [64, 512, 256], P('bx', 'by'), may hold values from 2 to 4
- send_index: int32 [32, 4, 32, 128], P('bx', 'by'), may hold values from 0 to 65535
- recv_index: int32 [32, 4, 32, 128], P('bx', 'by'), may hold values from 0 to 65535
- contact_live: int32 [32, 4, 32, 128], P('bx', 'by'), may hold values 0 or 1
Outputs:
- velocity_out: float32 [3, 64, 512, 256], P(None, 'bx', 'by')
- displacement_out: float32 [3, 64, 512, 256], P(None, 'bx', 'by')
- density_out: float32 [64, 512, 256], P('bx', 'by')
- energy_out: float32 [64, 512, 256], P('bx', 'by')
The draws below stay inside these ranges and needn't reach their ends.
All inputs are finite; a program needn't handle non-finite values. Where the reference program divides by a largest or mean magnitude, that divisor is 1e-20 or more. No bound on the sum of `contact_live` on one device may be relied on, other than what follows from the above.
Results may differ from the reference program's by a relative error of at most 0.00002.
Values sent between devices are 32-bit elements; how exact they have to be, the bound alone decides.
A program may use at most 128 MiB of HBM per device.

```python
import math
import jax
import jax.numpy as jnp
from jax import lax

CX = 2
CY = 128
NZ = 256
CONTACTS = 128
NX = 64
NY = 512
N_BX = 32
N_BY = 4


def plant(values, own_key, least, top_value):
    longest = values.shape.index(max(values.shape))
    spots = []
    for shift in (0, 1):
        where = [jax.random.randint(jax.random.fold_in(own_key, axis), (), 0, length) for axis, length in enumerate(values.shape)]
        where[longest] = (where[longest] + shift) % values.shape[longest]
        spots.append(tuple(where))
    return values.at[spots[0]].set(least).at[spots[1]].set(top_value)


def steps_of(stream_key, shape, split, low, high):
    loudness = 1.0
    for axis_at, blocks in split:
        steps = jax.random.uniform(jax.random.fold_in(jax.random.fold_in(stream_key, 6), axis_at), (blocks,), jnp.float32, low / len(split), high / len(split))
        loudness = loudness * jnp.repeat(jnp.exp(steps), shape[axis_at] // blocks).reshape((-1,) + (1,) * (len(shape) - 1 - axis_at))
    return loudness


def noise(stream_key, extent, width, bound, split=(), kind=jnp.bfloat16):
    loudness = steps_of(stream_key, extent, split, -0.22, 0.18) if split else 1.0
    result = jax.random.normal(stream_key, extent, jnp.float32) * width * loudness
    return jnp.minimum(jnp.maximum(result, -bound), bound).astype(kind)


def setup_inputs(seed: int = 0) -> dict:
    splits = jax.random.split(jax.random.key(seed), 8)
    return {
        "displacement": noise(splits[0], (3, NX, NY, NZ), 0.02, 0.06, ((1, 32), (2, 4)), jnp.float32),
        "velocity": noise(splits[1], (3, NX, NY, NZ), 0.5, 1.5, ((1, 32), (2, 4)), jnp.float32),
        "zone_mass": jnp.clip(jnp.exp(math.log(1.25) - 0.4462871 * jax.random.uniform(splits[2], (NX, NY, NZ), jnp.float32) ** steps_of(splits[2], (NX, NY, NZ), ((0, 32), (1, 4)), -0.2, 0.2)), 0.8, 1.25),
        "energy": jnp.clip(jnp.exp(math.log(4.0) - 0.6931472 * jax.random.uniform(splits[3], (NX, NY, NZ), jnp.float32) ** steps_of(splits[3], (NX, NY, NZ), ((0, 32), (1, 4)), -0.2, 0.2)), 2.0, 4.0),
        "send_index": plant(jax.random.randint(splits[4], (N_BX, N_BY, N_BX, CONTACTS), 0, CX * CY * NZ), jax.random.fold_in(splits[4], 1), 0, (CX * CY * NZ) - 1).astype(jnp.int32),
        "recv_index": plant(jax.random.randint(splits[5], (N_BX, N_BY, N_BX, CONTACTS), 0, CX * CY * NZ), jax.random.fold_in(splits[5], 1), 0, (CX * CY * NZ) - 1).astype(jnp.int32),
        "contact_live": plant((jax.random.randint(splits[6], (N_BX, N_BY, N_BX, CONTACTS), 0, 2) < 1).astype(jnp.int32), jax.random.fold_in(splits[6], 1), 0, 1),
    }


gas_gamma = 1.4
quad_visc = 1.0
linear_visc = 0.25
courant = 0.25
contact_weight = 0.5

def cross_product(left, right):
    return jnp.stack([left[1] * right[2] - left[2] * right[1], left[2] * right[0] - left[0] * right[2], left[0] * right[1] - left[1] * right[0]])

def inner_three(left, right):
    return left[0] * right[0] + left[1] * right[1] + left[2] * right[2]

def node_edges(extended):
    first_diff = extended[:, 1:, :, :] - extended[:, :-1, :, :]
    first_sum = first_diff[:, :, :-1] + first_diff[:, :, 1:]
    first_edge = 0.25 * (first_sum + jnp.roll(first_sum, -1, axis=3))
    second_diff = extended[:, :, 1:] - extended[:, :, :-1]
    second_sum = second_diff[:, :-1] + second_diff[:, 1:]
    second_edge = 0.25 * (second_sum + jnp.roll(second_sum, -1, axis=3))
    third_diff = jnp.roll(extended, -1, axis=3) - extended
    third_sum = third_diff[:, :-1] + third_diff[:, 1:]
    third_edge = 0.25 * (third_sum[:, :, :-1] + third_sum[:, :, 1:])
    return (first_edge, second_edge, third_edge)

def geometry(extended):
    first_edge, second_edge, third_edge = node_edges(extended)
    units = jnp.eye(3, dtype=jnp.float32)
    return (first_edge + units[0].reshape(3, 1, 1, 1), second_edge + units[1].reshape(3, 1, 1, 1), third_edge + units[2].reshape(3, 1, 1, 1))

def volume_of(extended):
    first_edge, second_edge, third_edge = geometry(extended)
    return inner_three(first_edge, cross_product(second_edge, third_edge))

def zone_state(nodes, masses, energies):
    first_edge, second_edge, third_edge = geometry(nodes[0:3])
    first_grad, second_grad, third_grad = node_edges(nodes[3:6])
    area_one = cross_product(second_edge, third_edge)
    area_two = cross_product(third_edge, first_edge)
    area_three = cross_product(first_edge, second_edge)
    volume = inner_three(first_edge, area_one)
    rate = inner_three(first_grad, area_one) + inner_three(second_grad, area_two) + inner_three(third_grad, area_three)
    density = masses / volume
    pressure = (gas_gamma - 1.0) * density * energies
    sound = jnp.sqrt(gas_gamma * (gas_gamma - 1.0) * energies)
    length = jnp.cbrt(volume)
    squeeze = jnp.minimum(rate / volume, 0.0)
    viscous = density * (quad_visc * length * length * squeeze * squeeze - linear_visc * length * sound * squeeze)
    stress = pressure + viscous
    strain = lax.optimization_barrier(jnp.max(jnp.abs(jnp.concatenate([first_grad, second_grad, third_grad], 0)), axis=0))
    limit = length / (sound + 4.0 * length * strain)
    quarter = 0.25 * stress
    panel = jnp.concatenate([quarter * area_one, quarter * area_two, quarter * area_three], 0)
    return (volume, stress, panel, limit)

def node_force(panel_ext):
    first_part = panel_ext[0:3]
    second_part = panel_ext[3:6]
    third_part = panel_ext[6:9]
    first_diff = first_part[:, :-1] - first_part[:, 1:]
    first_sum = first_diff[:, :, 1:] + first_diff[:, :, :-1]
    first_force = first_sum + jnp.roll(first_sum, 1, axis=3)
    second_diff = second_part[:, :, :-1] - second_part[:, :, 1:]
    second_sum = second_diff[:, 1:] + second_diff[:, :-1]
    second_force = second_sum + jnp.roll(second_sum, 1, axis=3)
    third_diff = jnp.roll(third_part, 1, axis=3) - third_part
    third_sum = third_diff[:, 1:] + third_diff[:, :-1]
    third_force = third_sum[:, :, 1:] + third_sum[:, :, :-1]
    return first_force + second_force + third_force

def node_mass(mass_ext):
    first_sum = mass_ext[1:] + mass_ext[:-1]
    second_sum = first_sum[:, 1:] + first_sum[:, :-1]
    return 0.125 * (second_sum + jnp.roll(second_sum, 1, axis=2))

def upper_extend(field):
    field = jnp.concatenate([field, field[:, :1]], 1)
    return jnp.concatenate([field, field[:, :, :1]], 2)

def lower_extend(field):
    field = jnp.concatenate([field[:, -1:], field], 1)
    return jnp.concatenate([field[:, :, -1:], field], 2)

def to_blocks(field):
    count = field.shape[0]
    return field.reshape(count, N_BX, CX, N_BY, CY, NZ).transpose(0, 1, 3, 2, 4, 5).reshape(count, N_BX, N_BY, CX * CY * NZ)

def from_blocks(blocks):
    count = blocks.shape[0]
    return blocks.reshape(count, N_BX, N_BY, CX, CY, NZ).transpose(0, 1, 3, 2, 4, 5).reshape(count, N_BX * CX, N_BY * CY, NZ)

def reference(displacement, velocity, zone_mass, energy, send_index, recv_index, contact_live):
    nodes = upper_extend(jnp.concatenate([displacement, velocity], 0))
    volume, stress, panel, limit = zone_state(nodes, zone_mass, energy)
    time_step = courant * jnp.min(limit)
    zones = lower_extend(jnp.concatenate([panel, zone_mass[None]], 0))
    force = node_force(zones[0:9])
    nodal = node_mass(zones[9])
    predicted = velocity + time_step * (force / nodal)
    blocks = to_blocks(jnp.concatenate([predicted, nodal[None]], 0))
    tile_grid = jnp.arange(N_BX, dtype=jnp.int32).reshape(N_BX, 1, 1, 1)
    row_grid = jnp.arange(N_BY, dtype=jnp.int32).reshape(1, N_BY, 1, 1)
    master = blocks[:, tile_grid, row_grid, send_index].transpose(0, 3, 2, 1, 4)
    slave = blocks[:, tile_grid, row_grid, recv_index]
    weight = contact_live.astype(jnp.float32) * contact_weight * master[3] / (master[3] + slave[3])
    change = weight * (master[0:3] - slave[0:3])
    moved_blocks = blocks[0:3].at[:, tile_grid, row_grid, recv_index].add(change)
    velocity_out = from_blocks(moved_blocks)
    displacement_out = displacement + time_step * velocity_out
    new_volume = volume_of(upper_extend(displacement_out))
    density_out = zone_mass / new_volume
    energy_out = energy - stress * (new_volume - volume) / zone_mass
    return (velocity_out, displacement_out, density_out, energy_out)
```

```python
import functools

import jax
import jax.numpy as jnp
from jax import lax
from jax.experimental import pallas as pl
from jax.experimental.pallas import tpu as pltpu
from jax.sharding import PartitionSpec as P

MESH = pl.DeviceIdType.MESH
F32 = jnp.float32
BF16 = jnp.bfloat16


def split(x):
    hi = x.astype(BF16)
    lo = (x - hi.astype(F32)).astype(BF16)
    return hi, lo


def cross(a, b):
    return (
        a[1] * b[2] - a[2] * b[1],
        a[2] * b[0] - a[0] * b[2],
        a[0] * b[1] - a[1] * b[0],
    )


def dot3(a, b):
    return a[0] * b[0] + a[1] * b[1] + a[2] * b[2]


def roll_up(x):
    return pltpu.roll(x, x.shape[1] - 1, axis=1)


def roll_down(x):
    return pltpu.roll(x, 1, axis=1)


def edges(ref, field, plane, r):
    low = ref[field, plane, pl.ds(r, 16), :]
    high = ref[field, plane + 1, pl.ds(r, 16), :]
    l0, l1 = low[0:8], low[1:9]
    h0, h1 = high[0:8], high[1:9]
    lb, hb = l0 + l1, h0 + h1
    u1 = hb - lb
    u2 = (l1 - l0) + (h1 - h0)
    u3 = lb + hb
    return u1 + roll_up(u1), u2 + roll_up(u2), roll_up(u3) - u3


def geometry(ref, plane, r):
    parts = [edges(ref, f, plane, r) for f in range(3)]
    e1 = [parts[f][0] for f in range(3)]
    e2 = [parts[f][1] for f in range(3)]
    e3 = [parts[f][2] for f in range(3)]
    e1[0] = e1[0] + 4.0
    e2[1] = e2[1] + 4.0
    e3[2] = e3[2] + 4.0
    return e1, e2, e3


def kernel(
    nbx, nby, cx, cy, nz, chunks,
    disp, vel, mass, ener, sidx, ridx, live,
    vel_o, disp_o, den_o, ene_o,
    nod, mas, ene, vol, strs, frc, pan, fups, fupr, rmass, mov, velb,
    sids, rids, lives, wbuf,
    zm, mrow, zs, srow, rs, tab, taba, acce, accl,
    snd_e, rcv_e, snd_l, rcv_l, gmx, gms, gmr,
    lsem, osem, ssem, rsem, ese, ere, esl, erl,
):
    X = lax.axis_index("bx")
    Y = lax.axis_index("by")
    xu, xd = lax.rem(X + 1, nbx), lax.rem(X + nbx - 1, nbx)
    yu, yd = lax.rem(Y + 1, nby), lax.rem(Y + nby - 1, nby)
    rows = cx * cy
    tiles = nbx // 2
    hrows = cy // chunks
    body = pl.ds(8, cy)

    barrier = pltpu.get_barrier_semaphore()
    for dev in ((xd, yd), (xd, yu), (xu, yd), (xu, yu)):
        pl.semaphore_signal(barrier, inc=1, device_id=dev, device_id_type=MESH)
    for d in range(1, nby):
        pl.semaphore_signal(barrier, inc=1, device_id=(X, lax.rem(Y + d, nby)), device_id_type=MESH)

    @pl.loop(1, nbx)
    def _(d):
        pl.semaphore_signal(barrier, inc=1, device_id=(lax.rem(X + d, nbx), Y), device_id_type=MESH)

    loads = [
        (disp, nod.at[0:3, 0:2, body]),
        (vel, nod.at[3:6, 0:2, body]),
        (mass, mas.at[1:3, body]),
        (ener, ene.at[:, body]),
        (sidx.at[0, 0], sids),
        (ridx.at[0, 0], rids),
        (live.at[0, 0], lives),
    ]
    loads = [pltpu.make_async_copy(s, d, lsem.at[i]) for i, (s, d) in enumerate(loads)]
    for c in loads:
        c.start()

    pl.semaphore_wait(barrier, 4 + nby - 1 + nbx - 1)

    def remote(src, dst, k, dev):
        return pltpu.make_async_remote_copy(
            src_ref=src, dst_ref=dst, send_sem=ssem.at[k], recv_sem=rsem.at[k],
            device_id=dev, device_id_type=MESH,
        )

    top, bottom = pl.ds(8 + cy, 8), pl.ds(0, 8)
    first, last = pl.ds(0, 8), pl.ds(cy - 8, 8)
    plan = [
        (mass.at[1], mas.at[0, body], (xu, Y)),
        (mass.at[1, last], mas.at[0, bottom], (xu, yu)),
        (mass.at[:, last], mas.at[1:3, bottom], (X, yu)),
        (ener.at[:, last], ene.at[:, bottom], (X, yu)),
        (disp.at[:, :, first], nod.at[0:3, 0:2, top], (X, yd)),
        (vel.at[:, :, first], nod.at[3:6, 0:2, top], (X, yd)),
        (disp.at[:, :, last], nod.at[0:3, 0:2, bottom], (X, yu)),
        (vel.at[:, :, last], nod.at[3:6, 0:2, bottom], (X, yu)),
        (disp.at[:, 0, last], nod.at[0:3, 2, bottom], (xd, yu)),
        (vel.at[:, 0, last], nod.at[3:6, 2, bottom], (xd, yu)),
        (disp.at[:, 0, first], nod.at[0:3, 2, top], (xd, yd)),
        (vel.at[:, 0, first], nod.at[3:6, 2, top], (xd, yd)),
    ]
    base = len(plan)
    for h in range(chunks):
        src, dst = pl.ds(h * hrows, hrows), pl.ds(8 + h * hrows, hrows)
        plan.append((disp.at[:, 0, src], nod.at[0:3, 2, dst], (xd, Y)))
        plan.append((vel.at[:, 0, src], nod.at[3:6, 2, dst], (xd, Y)))
    halo = [remote(s, d, k, dev) for k, (s, d, dev) in enumerate(plan)]
    for c in halo:
        c.start()
    upk = len(plan)
    up = []
    edge = [0] + [h * hrows - 8 for h in range(1, chunks)] + [cy]
    for h in range(chunks):
        cut = pl.ds(edge[h], edge[h + 1] - edge[h])
        up.append(remote(fups.at[:, cut], fupr.at[:, cut], upk + h, (xu, Y)))
    gmk = upk + chunks
    gm = [remote(gms, gmr.at[d - 1], gmk + d - 1, (X, lax.rem(Y + d, nby))) for d in range(1, nby)]
    lk = gmk + nby - 1
    late = [
        remote(mov.at[:, 0, body], mov.at[:, 2, body], lk, (xd, Y)),
        remote(mov.at[:, 0, pl.ds(8, 8)], mov.at[:, 2, top], lk + 1, (xd, yd)),
        remote(mov.at[:, 0:2, pl.ds(8, 8)], mov.at[:, 0:2, top], lk + 2, (X, yd)),
    ]

    def exchange(snd, rcv, s_sem, r_sem, d):
        to = lax.rem(X + d, nbx)
        return pltpu.make_async_remote_copy(
            src_ref=snd.at[to], dst_ref=rcv.at[X], send_sem=s_sem.at[d], recv_sem=r_sem.at[d],
            device_id=(to, Y), device_id_type=MESH,
        )

    def exchange_start(snd, rcv, s_sem, r_sem):
        @pl.loop(1, nbx)
        def _(d):
            exchange(snd, rcv, s_sem, r_sem, d).start()
        pltpu.make_async_copy(snd.at[X], rcv.at[X], r_sem.at[0]).start()

    def exchange_wait(snd, rcv, s_sem, r_sem):
        @pl.loop(1, nbx)
        def _(d):
            c = exchange(snd, rcv, s_sem, r_sem, d)
            c.wait_send()
            frm = lax.rem(X + nbx - d, nbx)
            pltpu.make_async_remote_copy(
                src_ref=snd.at[frm], dst_ref=rcv.at[frm], send_sem=s_sem.at[d], recv_sem=r_sem.at[d],
                device_id=(frm, Y), device_id_type=MESH,
            ).wait_recv()
        pltpu.make_async_copy(snd.at[X], rcv.at[X], r_sem.at[0]).wait()

    for c in loads[4:]:
        c.wait()
    shift = nz.bit_length() - 1

    def pair_row(ref, t):
        two = ref[pl.ds(2 * t, 2), :]
        return jnp.concatenate([two[0:1], two[1:2]], axis=1)

    @pl.loop(0, tiles)
    def _(t):
        for ids, z, row in ((sids, zm, mrow), (rids, zs, srow)):
            idx = pair_row(ids, t)
            col = jnp.bitwise_and(idx, nz - 1)
            r = lax.shift_right_logical(idx, shift)
            row[t] = r
            lane = lax.broadcasted_iota(jnp.int32, (nz, 256), 0)
            z[t] = jnp.where(lane == col, 1.0, 0.0).astype(BF16)
            if row is srow:
                line = lax.broadcasted_iota(jnp.int32, (rows, 256), 0)
                rs[t] = jnp.where(line == r, 1.0, 0.0).astype(BF16)

    def zone(z, r, carry):
        e1, e2, e3 = geometry(nod, z, r)
        grads = [edges(nod, 3 + f, z, r) for f in range(3)]
        g1 = [g[0] for g in grads]
        g2 = [g[1] for g in grads]
        g3 = [g[2] for g in grads]
        a1, a2, a3 = cross(e2, e3), cross(e3, e1), cross(e1, e2)
        v = dot3(e1, a1) * (1.0 / 64.0)
        rate = (dot3(g1, a1) + dot3(g2, a2) + dot3(g3, a3)) * (1.0 / 64.0)
        m = mas[z + 1, pl.ds(r, 8), :]
        e = ene[z, pl.ds(r, 8), :]
        rv = 1.0 / v
        rho = m * rv
        cs = jnp.sqrt(0.56 * e)
        length = jnp.exp(jnp.log(v) * (1.0 / 3.0))
        length = length + length * (v - length * length * length) * rv * (1.0 / 3.0)
        ld = length * jnp.minimum(rate * rv, 0.0)
        stress = rho * (0.4 * e + ld * (ld - 0.25 * cs))
        peak = jnp.abs(g1[0])
        for g in g1[1:] + g2 + g3:
            peak = jnp.maximum(peak, jnp.abs(g))
        inverse = cs * length * length * rv + peak
        k = stress * (1.0 / 64.0)
        vol[z, pl.ds(r, 8), :] = v
        strs[z, pl.ds(r, 8), :] = stress
        for f in range(3):
            p1, p2, p3 = k * a1[f], k * a2[f], k * a3[f]
            q1 = p1 + roll_down(p1)
            q2 = p2 + roll_down(p2)
            q3 = roll_down(p3) - p3
            pan[f, pl.ds(r, 8), :] = q3 - q1
            pan[3 + f, pl.ds(r, 8), :] = q3 + q1
            pan[6 + f, pl.ds(r, 8), :] = q2
        return jnp.maximum(carry, inverse)

    def force(z, r):
        for f in range(3):
            qm = pan[f, pl.ds(r - 8, 16), :]
            qp = pan[3 + f, pl.ds(r - 8, 16), :]
            q2 = pan[6 + f, pl.ds(r - 8, 16), :]
            here = slice(8, 16)
            back = slice(7, 15)
            turn = q2[back] - q2[here]
            lower = qm[here] + qm[back] + turn
            upper = qp[here] + qp[back] + turn
            at = pl.ds(r - 8, 8)
            if z == 0:
                frc[f, 0, at, :] = lower
                frc[f, 1, at, :] = upper
            else:
                frc[f, 1, at, :] = frc[f, 1, at, :] + lower
                fups[f, at, :] = upper

    def zones(z, lo, hi):
        def step(i, carry):
            r = pl.multiple_of(i * 8, 8)
            carry = zone(z, r, carry)

            @pl.when(i > 0)
            def _():
                force(z, r)
            return carry
        gmx[...] = lax.fori_loop(lo, hi, step, gmx[...])

    gmx[...] = jnp.zeros_like(gmx)
    for c in loads[:4]:
        c.wait()
    for c in halo[2:8]:
        c.wait()
    zones(0, 0, cy // 8 + 1)

    for c in halo[0:2]:
        c.wait()

    def early_table(i, _):
        b = pl.multiple_of(i * 16, 16)
        s = [mas[p, pl.ds(pl.multiple_of(8 + b - 8, 8), 24), :] for p in range(3)]
        for p in range(2):
            t = s[p] + s[p + 1]
            t = t[8:24] + t[7:23]
            m = 0.125 * (t + roll_down(t))
            rmass[p, pl.ds(b, 16), :] = 1.0 / m
            at = pl.multiple_of(p * cy + b, 16)
            for f in range(4):
                hi, lo = split(m if f == 3 else nod[3 + f, p, pl.ds(8 + b, 16), :])
                tab[0, pl.ds(f * rows + at, 16), :] = hi
                tab[1, pl.ds(f * rows + at, 16), :] = lo
        return 0
    lax.fori_loop(0, cy // 16, early_table, 0)

    def gather(table, start, fields, z, row, t):
        cut = pl.ds(start * rows, fields * rows)
        o = jnp.dot(table[0, cut, :], z[t], preferred_element_type=F32)
        o = o + jnp.dot(table[1, cut, :], z[t], preferred_element_type=F32)
        line = lax.broadcasted_iota(jnp.int32, (rows, 256), 0)
        hit = line == row[t]
        return [
            jnp.sum(jnp.where(hit, o[f * rows : (f + 1) * rows], 0.0), axis=0, keepdims=True)
            for f in range(fields)
        ]

    @pl.loop(0, tiles)
    def _(t):
        for f, g in enumerate(gather(tab, 0, 4, zm, mrow, t)):
            snd_e[2 * t, f : f + 1, :] = g[:, :128]
            snd_e[2 * t + 1, f : f + 1, :] = g[:, 128:]
    exchange_start(snd_e, rcv_e, ese, ere)

    def chunk_zones(h):
        halo[base + 2 * h].wait()
        halo[base + 2 * h + 1].wait()
        if h == 0:
            for c in halo[8:10]:
                c.wait()
        if h == chunks - 1:
            for c in halo[10:12]:
                c.wait()
        lo = 0 if h == 0 else h * hrows // 8
        hi = cy // 8 + 1 if h == chunks - 1 else (h + 1) * hrows // 8
        zones(1, lo, hi)

    chunk_zones(0)
    up[0].start()

    @pl.loop(0, tiles)
    def _(t):
        (g,) = gather(tab, 3, 1, zs, srow, t)
        wbuf[pl.ds(2 * t, 1), :] = g[:, :128]
        wbuf[pl.ds(2 * t + 1, 1), :] = g[:, 128:]

    exchange_wait(snd_e, rcv_e, ese, ere)

    def scatter(acc, values, t):
        fields = len(values)
        parts = ([], [])
        for v in values:
            for side, piece in zip(parts, split(v)):
                side.append(rs[t] * piece)
        o = None
        for side in parts:
            lhs = jnp.concatenate(side, axis=0)
            d = lax.dot_general(lhs, zs[t], (((1,), (1,)), ((), ())), preferred_element_type=F32)
            o = d if o is None else o + d
        acc[...] = acc[...] + o

    def pair_field(rcv, f, t):
        return jnp.concatenate([rcv[2 * t, f : f + 1, :], rcv[2 * t + 1, f : f + 1, :]], axis=1)

    acce[...] = jnp.zeros_like(acce)

    @pl.loop(0, tiles)
    def _(t):
        mm = pair_field(rcv_e, 3, t)
        ms = pair_row(wbuf, t)
        w = pair_row(lives, t).astype(F32) * 0.5 * mm / (mm + ms)
        wbuf[pl.ds(2 * t, 1), :] = w[:, :128]
        wbuf[pl.ds(2 * t + 1, 1), :] = w[:, 128:]
        scatter(acce, [w * pair_field(rcv_e, f, t) for f in range(3)] + [w], t)

    for h in range(1, chunks):
        chunk_zones(h)
        up[h].start()

    gms[...] = gmx[:, :128]
    for b in range(128, nz, 128):
        gms[...] = jnp.maximum(gms[...], gmx[:, b : b + 128])
    for c in gm:
        c.start()

    for c in up:
        c.wait()

    def accel(i, _):
        b = pl.multiple_of(i * 16, 16)
        for p in range(2):
            rm = rmass[p, pl.ds(b, 16), :]
            at = pl.multiple_of(p * cy + b, 16)
            for f in range(3):
                a = frc[f, p, pl.ds(b, 16), :]
                if p == 0:
                    a = a + fupr[f, pl.ds(b, 16), :]
                a = a * rm
                frc[f, p, pl.ds(b, 16), :] = a
                hi, lo = split(a)
                taba[0, pl.ds(f * rows + at, 16), :] = hi
                taba[1, pl.ds(f * rows + at, 16), :] = lo
        return 0
    lax.fori_loop(0, cy // 16, accel, 0)

    @pl.loop(0, tiles)
    def _(t):
        for f, g in enumerate(gather(taba, 0, 3, zm, mrow, t)):
            snd_l[2 * t, f : f + 1, :] = g[:, :128]
            snd_l[2 * t + 1, f : f + 1, :] = g[:, 128:]

    for c in gm:
        c.wait()
    g = gms[...]
    for d in range(1, nby):
        g = jnp.maximum(g, gmr[d - 1])
    g = jnp.max(jnp.max(g, axis=0, keepdims=True), axis=1, keepdims=True)
    g = jnp.broadcast_to(g, (1, 128))

    @pl.loop(0, nbx)
    def _(d):
        snd_l[d, 3:4, :] = g
    exchange_start(snd_l, rcv_l, esl, erl)
    accl[...] = jnp.zeros_like(accl)
    exchange_wait(snd_l, rcv_l, esl, erl)

    @pl.loop(0, tiles)
    def _(t):
        w = pair_row(wbuf, t)
        scatter(accl, [w * pair_field(rcv_l, f, t) for f in range(3)], t)

    g = lax.fori_loop(0, nbx, lambda d, c: jnp.maximum(c, rcv_l[d]), rcv_l[0])
    dt = 0.25 / jnp.broadcast_to(g[3:4, 0:1], (8, nz))

    def move(p):
        def step(i, _):
            b = pl.multiple_of(i * 8, 8)
            at = pl.multiple_of(p * cy + b, 8)
            keep = 1.0 - acce[pl.ds(3 * rows + at, 8), :]
            for f in range(3):
                v = nod[3 + f, p, pl.ds(8 + b, 8), :] + dt * frc[f, p, pl.ds(b, 8), :]
                v = v * keep + (acce[pl.ds(f * rows + at, 8), :] + dt * accl[pl.ds(f * rows + at, 8), :])
                velb[f, p, pl.ds(b, 8), :] = v
                mov[f, p, pl.ds(8 + b, 8), :] = nod[f, p, pl.ds(8 + b, 8), :] + dt * v
            return 0
        lax.fori_loop(0, cy // 8, step, 0)

    move(0)
    late[0].start()
    late[1].start()
    move(1)
    late[2].start()
    outs = [
        pltpu.make_async_copy(velb, vel_o, osem.at[0]),
        pltpu.make_async_copy(mov.at[:, 0:2, body], disp_o, osem.at[1]),
    ]
    for c in outs:
        c.start()

    def finish(p):
        def step(i, _):
            b = pl.multiple_of(i * 8, 8)
            r = pl.multiple_of(8 + b, 8)
            e1, e2, e3 = geometry(mov, p, r)
            v = dot3(e1, cross(e2, e3)) * (1.0 / 64.0)
            m = mas[p + 1, pl.ds(r, 8), :]
            den_o[p, pl.ds(b, 8), :] = m / v
            change = v - vol[p, pl.ds(r, 8), :]
            ene_o[p, pl.ds(b, 8), :] = ene[p, pl.ds(r, 8), :] - strs[p, pl.ds(r, 8), :] * change / m
            return 0
        lax.fori_loop(0, cy // 8, step, 0)

    late[2].wait()
    finish(0)
    late[0].wait()
    late[1].wait()
    finish(1)
    for c in outs:
        c.wait()


def solution(mesh):
    nbx, nby = mesh.shape["bx"], mesh.shape["by"]

    def local(displacement, velocity, zone_mass, energy, send_index, recv_index, contact_live):
        _, cx, cy, nz = displacement.shape
        rows = cx * cy
        chunks = 4 if cy >= 64 else 2
        tiles = nbx // 2
        tall = cy + 16
        copies = 12 + 2 * chunks + chunks + nby - 1 + 3
        anywhere = pl.BlockSpec(memory_space=pl.ANY)
        inside = pl.BlockSpec(memory_space=pltpu.VMEM)
        V = pltpu.VMEM
        scratch = [
            V((6, 3, tall, nz), F32),
            V((3, cy + 8, nz), F32),
            V((cx, cy + 8, nz), F32),
            V((cx, cy + 8, nz), F32),
            V((cx, cy + 8, nz), F32),
            V((3, cx, cy, nz), F32),
            V((9, cy + 8, nz), F32),
            V((3, cy, nz), F32),
            V((3, cy, nz), F32),
            V((cx, cy, nz), F32),
            V((3, 3, tall, nz), F32),
            V((3, cx, cy, nz), F32),
            V((nbx, 128), jnp.int32),
            V((nbx, 128), jnp.int32),
            V((nbx, 128), jnp.int32),
            V((nbx, 128), F32),
            V((tiles, nz, 256), BF16),
            V((tiles, 1, 256), jnp.int32),
            V((tiles, nz, 256), BF16),
            V((tiles, 1, 256), jnp.int32),
            V((tiles, rows, 256), BF16),
            V((2, 4 * rows, nz), BF16),
            V((2, 3 * rows, nz), BF16),
            V((4 * rows, nz), F32),
            V((3 * rows, nz), F32),
            V((nbx, 4, 128), F32),
            V((nbx, 4, 128), F32),
            V((nbx, 4, 128), F32),
            V((nbx, 4, 128), F32),
            V((8, nz), F32),
            V((8, 128), F32),
            V((nby - 1, 8, 128), F32),
            pltpu.SemaphoreType.DMA((7,)),
            pltpu.SemaphoreType.DMA((2,)),
            pltpu.SemaphoreType.DMA((copies,)),
            pltpu.SemaphoreType.DMA((copies,)),
            pltpu.SemaphoreType.DMA((nbx,)),
            pltpu.SemaphoreType.DMA((nbx,)),
            pltpu.SemaphoreType.DMA((nbx,)),
            pltpu.SemaphoreType.DMA((nbx,)),
        ]
        return pl.pallas_call(
            functools.partial(kernel, nbx, nby, cx, cy, nz, chunks),
            out_shape=(
                jax.ShapeDtypeStruct(displacement.shape, F32),
                jax.ShapeDtypeStruct(displacement.shape, F32),
                jax.ShapeDtypeStruct(zone_mass.shape, F32),
                jax.ShapeDtypeStruct(zone_mass.shape, F32),
            ),
            in_specs=[anywhere] * 7,
            out_specs=(anywhere, anywhere, inside, inside),
            scratch_shapes=scratch,
            compiler_params=pltpu.CompilerParams(
                collective_id=0, has_side_effects=True, vmem_limit_bytes=60 * 1024 * 1024
            ),
        )(displacement, velocity, zone_mass, energy, send_index, recv_index, contact_live)

    field = P(None, "bx", "by", None)
    flat = P("bx", "by", None)
    panel = P("bx", "by", None, None)
    return jax.shard_map(
        local,
        mesh=mesh,
        in_specs=(field, field, flat, flat, panel, panel, panel),
        out_specs=(field, field, flat, flat),
        check_vma=False,
    )
```

```python
import functools

import jax
import jax.numpy as jnp
from jax import lax
from jax.experimental import pallas as pl
from jax.experimental.pallas import tpu as pltpu
from jax.sharding import PartitionSpec as P

MESH = pl.DeviceIdType.MESH
F32 = jnp.float32
BF16 = jnp.bfloat16


def split(x):
    hi = x.astype(BF16)
    lo = (x - hi.astype(F32)).astype(BF16)
    return hi, lo


def cross(a, b):
    return (
        a[1] * b[2] - a[2] * b[1],
        a[2] * b[0] - a[0] * b[2],
        a[0] * b[1] - a[1] * b[0],
    )


def dot3(a, b):
    return a[0] * b[0] + a[1] * b[1] + a[2] * b[2]


def roll_up(x):
    return pltpu.roll(x, x.shape[1] - 1, axis=1)


def roll_down(x):
    return pltpu.roll(x, 1, axis=1)


def edges(ref, field, plane, r):
    low = ref[field, plane, pl.ds(r, 16), :]
    high = ref[field, plane + 1, pl.ds(r, 16), :]
    l0, l1 = low[0:8], low[1:9]
    h0, h1 = high[0:8], high[1:9]
    lb, hb = l0 + l1, h0 + h1
    u1 = hb - lb
    u2 = (l1 - l0) + (h1 - h0)
    u3 = lb + hb
    return u1 + roll_up(u1), u2 + roll_up(u2), roll_up(u3) - u3


def geometry(ref, plane, r):
    parts = [edges(ref, f, plane, r) for f in range(3)]
    e1 = [parts[f][0] for f in range(3)]
    e2 = [parts[f][1] for f in range(3)]
    e3 = [parts[f][2] for f in range(3)]
    e1[0] = e1[0] + 4.0
    e2[1] = e2[1] + 4.0
    e3[2] = e3[2] + 4.0
    return e1, e2, e3


def finish(mov, plane, r, m, e, v0, stress):
    e1, e2, e3 = geometry(mov, plane, r)
    v = dot3(e1, cross(e2, e3)) * (1.0 / 64.0)
    rm = 1.0 / m
    return m / v, e - stress * (v - v0) * rm


def kernel(
    nbx, nby, cx, cy, nz, bounds,
    disp, vel, mass, ener, sidx, ridx, live,
    vel_x, mov_x, fin_x, old_x,
    nod, mas, ene, old, fin, frc, pan, fups, fupr, rmass, mov, velb,
    sids, rids, lives, wbuf,
    zm, mrow, zs, srow, rs, tab, taba, acce, accl,
    snd_e, rcv_e, snd_l, rcv_l, gmx, gms, gmr, gsx, gall,
    lsem, osem, ssem, rsem, ese, ere, esl, erl, esg, erg,
):
    X = lax.axis_index("bx")
    Y = lax.axis_index("by")
    xu, xd = lax.rem(X + 1, nbx), lax.rem(X + nbx - 1, nbx)
    yu, yd = lax.rem(Y + 1, nby), lax.rem(Y + nby - 1, nby)
    rows = cx * cy
    tiles = nbx // 2
    wide = nbx // 4
    chunks = len(bounds) - 1
    body = pl.ds(8, cy)

    barrier = pltpu.get_barrier_semaphore()
    for dev in ((xd, yd), (xd, yu), (xu, yd), (xu, yu)):
        pl.semaphore_signal(barrier, inc=1, device_id=dev, device_id_type=MESH)
    for d in range(1, nby):
        pl.semaphore_signal(barrier, inc=1, device_id=(X, lax.rem(Y + d, nby)), device_id_type=MESH)

    @pl.loop(1, nbx)
    def _(d):
        pl.semaphore_signal(barrier, inc=1, device_id=(lax.rem(X + d, nbx), Y), device_id_type=MESH)

    loads = [
        (sidx.at[0, 0], sids),
        (ridx.at[0, 0], rids),
        (live.at[0, 0], lives),
        (disp, nod.at[0:3, 0:2, body]),
        (vel, nod.at[3:6, 0:2, body]),
        (mass, mas.at[1:3, body]),
        (ener, ene.at[:, body]),
    ]
    loads = [pltpu.make_async_copy(s, d, lsem.at[i]) for i, (s, d) in enumerate(loads)]
    for c in loads:
        c.start()

    pl.semaphore_wait(barrier, 4 + nby - 1 + nbx - 1)

    def remote(src, dst, k, dev):
        return pltpu.make_async_remote_copy(
            src_ref=src, dst_ref=dst, send_sem=ssem.at[k], recv_sem=rsem.at[k],
            device_id=dev, device_id_type=MESH,
        )

    top, bottom = pl.ds(8 + cy, 8), pl.ds(0, 8)
    first, last = pl.ds(0, 8), pl.ds(cy - 8, 8)
    plan = [
        (mass.at[1], mas.at[0, body], (xu, Y)),
        (mass.at[1, last], mas.at[0, bottom], (xu, yu)),
        (mass.at[:, last], mas.at[1:3, bottom], (X, yu)),
        (ener.at[:, last], ene.at[:, bottom], (X, yu)),
        (disp.at[:, :, first], nod.at[0:3, 0:2, top], (X, yd)),
        (vel.at[:, :, first], nod.at[3:6, 0:2, top], (X, yd)),
        (disp.at[:, :, last], nod.at[0:3, 0:2, bottom], (X, yu)),
        (vel.at[:, :, last], nod.at[3:6, 0:2, bottom], (X, yu)),
        (disp.at[:, 0, last], nod.at[0:3, 2, bottom], (xd, yu)),
        (vel.at[:, 0, last], nod.at[3:6, 2, bottom], (xd, yu)),
        (disp.at[:, 0, first], nod.at[0:3, 2, top], (xd, yd)),
        (vel.at[:, 0, first], nod.at[3:6, 2, top], (xd, yd)),
    ]
    base = len(plan)
    for h in range(chunks):
        src, dst = pl.ds(bounds[h], bounds[h + 1] - bounds[h]), pl.ds(8 + bounds[h], bounds[h + 1] - bounds[h])
        plan.append((disp.at[:, 0, src], nod.at[0:3, 2, dst], (xd, Y)))
        plan.append((vel.at[:, 0, src], nod.at[3:6, 2, dst], (xd, Y)))
    halo = [remote(s, d, k, dev) for k, (s, d, dev) in enumerate(plan)]
    for c in halo:
        c.start()
    upk = len(plan)
    up = []
    edge = [0] + [b - 8 for b in bounds[1:-1]] + [cy]
    for h in range(chunks):
        cut = pl.ds(edge[h], edge[h + 1] - edge[h])
        up.append(remote(fups.at[:, cut], fupr.at[:, cut], upk + h, (xu, Y)))
    gmk = upk + chunks
    gm = [remote(gms, gmr.at[d - 1], gmk + d - 1, (X, lax.rem(Y + d, nby))) for d in range(1, nby)]
    lk = gmk + nby - 1
    late = [
        remote(mov.at[:, 0, body], mov.at[:, 2, body], lk, (xd, Y)),
        remote(mov.at[:, 0, pl.ds(8, 8)], mov.at[:, 2, top], lk + 1, (xd, yd)),
        remote(mov.at[:, 0, pl.ds(8, 8)], mov.at[:, 0, top], lk + 2, (X, yd)),
        remote(mov.at[:, 1, pl.ds(8, 8)], mov.at[:, 1, top], lk + 3, (X, yd)),
    ]

    def sending(snd, rcv, s_sem, r_sem, to, d):
        return pltpu.make_async_remote_copy(
            src_ref=snd, dst_ref=rcv.at[X], send_sem=s_sem.at[d], recv_sem=r_sem.at[d],
            device_id=(to, Y), device_id_type=MESH,
        )

    def arriving(snd, rcv, s_sem, r_sem, frm):
        d = lax.rem(X - frm + nbx, nbx)
        return pltpu.make_async_remote_copy(
            src_ref=snd, dst_ref=rcv.at[frm], send_sem=s_sem.at[d], recv_sem=r_sem.at[d],
            device_id=(frm, Y), device_id_type=MESH,
        )

    for c in loads[:3]:
        c.wait()
    shift = nz.bit_length() - 1

    def line_up(ref, t, count):
        return jnp.concatenate([ref[pl.ds(count * t + i, 1), :] for i in range(count)], axis=1)

    def hot(length, index):
        line = lax.broadcasted_iota(jnp.int32, (length, index.shape[1]), 0)
        return jnp.where(line == index, 1.0, 0.0).astype(BF16)

    @pl.loop(0, tiles)
    def _(t):
        idx = line_up(sids, t, 2)
        mrow[t] = lax.shift_right_logical(idx, shift)
        zm[t] = hot(nz, jnp.bitwise_and(idx, nz - 1))

    @pl.loop(0, wide)
    def _(t):
        idx = line_up(rids, t, 4)
        row = lax.shift_right_logical(idx, shift)
        srow[t] = row
        zs[t] = hot(nz, jnp.bitwise_and(idx, nz - 1))
        rs[t] = hot(rows, row)

    def zone(z, r, carry):
        e1, e2, e3 = geometry(nod, z, r)
        grads = [edges(nod, 3 + f, z, r) for f in range(3)]
        g1 = [g[0] for g in grads]
        g2 = [g[1] for g in grads]
        g3 = [g[2] for g in grads]
        a1, a2, a3 = cross(e2, e3), cross(e3, e1), cross(e1, e2)
        v = dot3(e1, a1) * (1.0 / 64.0)
        rate = (dot3(g1, a1) + dot3(g2, a2) + dot3(g3, a3)) * (1.0 / 64.0)
        m = mas[z + 1, pl.ds(r, 8), :]
        e = ene[z, pl.ds(r, 8), :]
        rv = 1.0 / v
        rho = m * rv
        cs = jnp.sqrt(0.56 * e)
        length = jnp.exp(jnp.log(v) * (1.0 / 3.0))
        length = length + length * (v - length * length * length) * rv * (1.0 / 3.0)
        ld = length * jnp.minimum(rate * rv, 0.0)
        stress = rho * (0.4 * e + ld * (ld - 0.25 * cs))
        peak = jnp.abs(g1[0])
        for g in g1[1:] + g2 + g3:
            peak = jnp.maximum(peak, jnp.abs(g))
        inverse = cs * length * length * rv + peak
        k = stress * (1.0 / 64.0)
        old[0, z, pl.ds(r, 8), :] = v
        old[1, z, pl.ds(r, 8), :] = stress
        for f in range(3):
            p1, p2, p3 = k * a1[f], k * a2[f], k * a3[f]
            q1 = p1 + roll_down(p1)
            q2 = p2 + roll_down(p2)
            q3 = roll_down(p3) - p3
            pan[f, pl.ds(r, 8), :] = q3 - q1
            pan[3 + f, pl.ds(r, 8), :] = q3 + q1
            pan[6 + f, pl.ds(r, 8), :] = q2
        return jnp.maximum(carry, inverse)

    def force(z, r):
        for f in range(3):
            qm = pan[f, pl.ds(r - 8, 16), :]
            qp = pan[3 + f, pl.ds(r - 8, 16), :]
            q2 = pan[6 + f, pl.ds(r - 8, 16), :]
            here = slice(8, 16)
            back = slice(7, 15)
            turn = q2[back] - q2[here]
            lower = qm[here] + qm[back] + turn
            upper = qp[here] + qp[back] + turn
            at = pl.ds(r - 8, 8)
            if z == 0:
                frc[f, 0, at, :] = lower
                frc[f, 1, at, :] = upper
            else:
                frc[f, 1, at, :] = frc[f, 1, at, :] + lower
                fups[f, at, :] = upper

    def zones(z, lo, hi):
        def step(i, carry):
            r = pl.multiple_of(i * 8, 8)
            carry = zone(z, r, carry)

            @pl.when(i > 0)
            def _():
                force(z, r)
            return carry
        gmx[...] = lax.fori_loop(lo, hi, step, gmx[...])

    gmx[...] = jnp.zeros_like(gmx)
    for c in loads[3:]:
        c.wait()
    for c in halo[2:8]:
        c.wait()
    zones(0, 0, cy // 8 + 1)

    for c in halo[0:2]:
        c.wait()

    @pl.loop(0, cy // 16)
    def _(i):
        b = pl.multiple_of(i * 16, 16)
        s = [mas[p, pl.ds(b, 24), :] for p in range(3)]
        for p in range(2):
            t = s[p] + s[p + 1]
            t = t[8:24] + t[7:23]
            m = 0.125 * (t + roll_down(t))
            rmass[p, pl.ds(b, 16), :] = 1.0 / m
            at = pl.multiple_of(p * cy + b, 16)
            for f in range(4):
                hi, lo = split(m if f == 3 else nod[3 + f, p, pl.ds(8 + b, 16), :])
                tab[0, pl.ds(f * rows + at, 16), :] = hi
                tab[1, pl.ds(f * rows + at, 16), :] = lo

    def gather(high, low, z, row, length):
        o = jnp.dot(high, z, preferred_element_type=F32)
        o = o + jnp.dot(low, z, preferred_element_type=F32)
        hit = lax.broadcasted_iota(jnp.int32, (length, z.shape[1]), 0) == row
        return [
            jnp.sum(jnp.where(hit, o[b : b + length], 0.0), axis=0, keepdims=True)
            for b in range(0, o.shape[0], length)
        ]

    @pl.loop(0, tiles)
    def _(t):
        for f, g in enumerate(gather(tab[0], tab[1], zm[t], mrow[t], rows)):
            snd_e[2 * t, f : f + 1, :] = g[:, :128]
            snd_e[2 * t + 1, f : f + 1, :] = g[:, 128:]

    @pl.loop(1, nbx)
    def _(d):
        to = lax.rem(X + d, nbx)
        sending(snd_e.at[to], rcv_e, ese, ere, to, d).start()
    rcv_e[X] = snd_e[X]

    def chunk_zones(h):
        halo[base + 2 * h].wait()
        halo[base + 2 * h + 1].wait()
        if h == 0:
            for c in halo[8:10]:
                c.wait()
        if h == chunks - 1:
            for c in halo[10:12]:
                c.wait()
        lo = 0 if h == 0 else bounds[h] // 8
        hi = cy // 8 + 1 if h == chunks - 1 else bounds[h + 1] // 8
        zones(1, lo, hi)
        up[h].start()

    for h in range(chunks - 1):
        chunk_zones(h)

    cut = pl.ds(3 * rows, rows)

    @pl.loop(0, wide)
    def _(t):
        (g,) = gather(tab[0, cut, :], tab[1, cut, :], zs[t], srow[t], rows)
        for i in range(4):
            wbuf[pl.ds(4 * t + i, 1), :] = g[:, 128 * i : 128 * i + 128]

    @pl.loop(1, nbx)
    def _(d):
        to = lax.rem(X + d, nbx)
        sending(snd_e.at[to], rcv_e, ese, ere, to, d).wait_send()
        frm = lax.rem(X + nbx - d, nbx)
        arriving(snd_e.at[frm], rcv_e, ese, ere, frm).wait_recv()

    @pl.loop(0, nbx)
    def _(s):
        mm = rcv_e[s, 3:4, :]
        ms = wbuf[pl.ds(s, 1), :]
        wbuf[pl.ds(s, 1), :] = lives[pl.ds(s, 1), :].astype(F32) * 0.5 * mm / (mm + ms)

    chunk_zones(chunks - 1)

    peak = gmx[:, :128]
    for b in range(128, nz, 128):
        peak = jnp.maximum(peak, gmx[:, b : b + 128])
    gms[...] = peak
    for c in gm:
        c.start()

    def accel(p):
        @pl.loop(0, cy // 16)
        def _(i):
            b = pl.multiple_of(i * 16, 16)
            rm = rmass[p, pl.ds(b, 16), :]
            for f in range(3):
                a = frc[f, p, pl.ds(b, 16), :]
                if p == 0:
                    a = a + fupr[f, pl.ds(b, 16), :]
                a = a * rm
                frc[f, p, pl.ds(b, 16), :] = a
                hi, lo = split(a)
                at = pl.ds(pl.multiple_of(f * cy + b, 16), 16)
                taba[0, p, at, :] = hi
                taba[1, p, at, :] = lo

    accel(1)

    def scatter(acc, rhs, hits, values):
        parts = ([], [])
        for v in values:
            for side, piece in zip(parts, split(v)):
                side.append(hits * piece)
        o = acc[...]
        for side in parts:
            lhs = side[0] if len(side) == 1 else jnp.concatenate(side, axis=0)
            o = o + lax.dot_general(lhs, rhs, (((1,), (1,)), ((), ())), preferred_element_type=F32)
        acc[...] = o

    acce[...] = jnp.zeros_like(acce)

    @pl.loop(0, wide)
    def _(t):
        scatter(acce, zs[t], rs[t], [line_up(wbuf, t, 4)])

    for c in gm:
        c.wait()
    g = gms[...]
    for d in range(1, nby):
        g = jnp.maximum(g, gmr[d - 1])
    gsx[...] = g
    gall[X] = g

    @pl.loop(1, nbx)
    def _(d):
        sending(gsx, gall, esg, erg, lax.rem(X + d, nbx), d).start()

    @pl.loop(0, tiles)
    def _(t):
        for f, g in enumerate(gather(taba[0, 1], taba[1, 1], zm[t], mrow[t] - cy, cy)):
            snd_l[2 * t, f : f + 1, :] = g[:, :128]
            snd_l[2 * t + 1, f : f + 1, :] = g[:, 128:]

    for c in up:
        c.wait()
    accel(0)
    mine = X // 2

    @pl.loop(0, tiles)
    def _(i):
        t = lax.rem(i + mine, tiles)
        for f, g in enumerate(gather(taba[0, 0], taba[1, 0], zm[t], mrow[t], cy)):
            snd_l[2 * t, f : f + 1, :] = snd_l[2 * t, f : f + 1, :] + g[:, :128]
            snd_l[2 * t + 1, f : f + 1, :] = snd_l[2 * t + 1, f : f + 1, :] + g[:, 128:]
        for k in range(2):
            to = 2 * t + k

            @pl.when(to != X)
            def _():
                sending(snd_l.at[to], rcv_l, esl, erl, to, lax.rem(to - X + nbx, nbx)).start()
    rcv_l[X] = snd_l[X]

    @pl.loop(1, nbx)
    def _(d):
        sending(gsx, gall, esg, erg, lax.rem(X + d, nbx), d).wait_send()
        arriving(gsx, gall, esg, erg, lax.rem(X + nbx - d, nbx)).wait_recv()
    g = lax.fori_loop(1, nbx, lambda d, c: jnp.maximum(c, gall[d]), gall[0])
    g = jnp.max(jnp.max(g, axis=0, keepdims=True), axis=1, keepdims=True)
    dt = 0.25 / jnp.broadcast_to(g, (8, nz))
    dt_row = dt[0:1, 0:128]

    accl[...] = jnp.zeros_like(accl)

    def late_scatter(p):
        @pl.loop(0, wide)
        def _(i):
            t = lax.rem(X // 4 - i + wide, wide)
            if p == 0:
                for k in range(4):
                    frm = 4 * t + k

                    @pl.when(frm != X)
                    def _():
                        arriving(snd_l.at[frm], rcv_l, esl, erl, frm).wait_recv()
            w = line_up(wbuf, t, 4)
            values = []
            for f in range(3):
                moved = [
                    rcv_e[4 * t + k, f : f + 1, :] + dt_row * rcv_l[4 * t + k, f : f + 1, :]
                    for k in range(4)
                ]
                values.append(w * jnp.concatenate(moved, axis=1))
            scatter(accl.at[p], zs[t], rs[t, p * cy : (p + 1) * cy, :], values)

    def move(p):
        @pl.loop(0, cy // 8)
        def _(i):
            b = pl.multiple_of(i * 8, 8)
            at = pl.multiple_of(p * cy + b, 8)
            keep = 1.0 - acce[pl.ds(at, 8), :]
            for f in range(3):
                v = nod[3 + f, p, pl.ds(8 + b, 8), :] + dt * frc[f, p, pl.ds(b, 8), :]
                v = v * keep + accl[p, pl.ds(pl.multiple_of(f * cy + b, 8), 8), :]
                velb[f, p, pl.ds(b, 8), :] = v
                mov[f, p, pl.ds(8 + b, 8), :] = nod[f, p, pl.ds(8 + b, 8), :] + dt * v

    late_scatter(0)
    move(0)
    for c in late[:3]:
        c.start()
    late_scatter(1)
    move(1)
    late[3].start()
    outs = [
        pltpu.make_async_copy(velb, vel_x, osem.at[0]),
        pltpu.make_async_copy(old.at[:, 1, body], old_x, osem.at[1]),
        pltpu.make_async_copy(mov.at[:, 0, body], mov_x.at[:, 0, body], osem.at[2]),
        pltpu.make_async_copy(mov.at[:, 1, body], mov_x.at[:, 1, body], osem.at[3]),
    ]
    for c in outs:
        c.start()

    @pl.loop(1, nbx)
    def _(d):
        to = lax.rem(X + d, nbx)
        sending(snd_l.at[to], rcv_l, esl, erl, to, d).wait_send()

    late[2].wait()
    late[3].wait()

    @pl.loop(0, cy // 8)
    def _(i):
        b = pl.multiple_of(i * 8, 8)
        r = pl.multiple_of(8 + b, 8)
        at = pl.ds(r, 8)
        d, e = finish(mov, 0, r, mas[1, at, :], ene[0, at, :], old[0, 0, at, :], old[1, 0, at, :])
        fin[0, pl.ds(b, 8), :] = d
        fin[1, pl.ds(b, 8), :] = e
    ends = [
        pltpu.make_async_copy(fin, fin_x, osem.at[4]),
        pltpu.make_async_copy(mov.at[:, 1, top], mov_x.at[:, 1, top], osem.at[5]),
        pltpu.make_async_copy(mov.at[:, 2, pl.ds(8, cy + 8)], mov_x.at[:, 2, pl.ds(8, cy + 8)], osem.at[6]),
    ]
    ends[0].start()
    ends[1].start()
    late[0].wait()
    late[1].wait()
    ends[2].start()
    for c in outs + ends:
        c.wait()


def write_out(
    cy, nz, vel_x, mov_x, fin_x, old_x, mass, ener, vel_o, disp_o, den_o, ene_o,
    velb, mov, fin, old, mas, ene, res, isem, osem,
):
    body = pl.ds(8, cy)
    ins = [
        (mov_x.at[:, 1, pl.ds(8, cy + 8)], mov.at[:, 1, pl.ds(8, cy + 8)]),
        (mov_x.at[:, 2, pl.ds(8, cy + 8)], mov.at[:, 2, pl.ds(8, cy + 8)]),
        (old_x, old),
        (mass.at[1], mas),
        (ener.at[1], ene),
        (mov_x.at[:, 0, body], mov.at[:, 0, body]),
        (vel_x, velb),
        (fin_x, fin),
    ]
    ins = [pltpu.make_async_copy(s, d, isem.at[i]) for i, (s, d) in enumerate(ins)]
    for c in ins:
        c.start()
    for c in ins[:5]:
        c.wait()

    def step(i, _):
        b = pl.multiple_of(i * 8, 8)
        at = pl.ds(b, 8)
        d, e = finish(
            mov, 1, pl.multiple_of(8 + b, 8), mas[at, :], ene[at, :], old[0, at, :], old[1, at, :]
        )
        res[0, at, :] = d
        res[1, at, :] = e
        return 0

    half = cy // 16
    lax.fori_loop(0, half, step, 0)
    for c in ins[5:]:
        c.wait()
    outs = [
        (velb, vel_o),
        (mov.at[:, 0:2, body], disp_o),
        (fin.at[0], den_o.at[0]),
        (fin.at[1], ene_o.at[0]),
        (res.at[0], den_o.at[1]),
        (res.at[1], ene_o.at[1]),
    ]
    outs = [pltpu.make_async_copy(s, d, osem.at[i]) for i, (s, d) in enumerate(outs)]
    for c in outs[:4]:
        c.start()
    lax.fori_loop(half, cy // 8, step, 0)
    for c in outs[4:]:
        c.start()
    for c in outs:
        c.wait()


def solution(mesh):
    nbx, nby = mesh.shape["bx"], mesh.shape["by"]

    def local(displacement, velocity, zone_mass, energy, send_index, recv_index, contact_live):
        _, cx, cy, nz = displacement.shape
        rows = cx * cy
        bounds = (0, 48, 88, 112, 128) if cy == 128 else (0, cy // 2, cy)
        chunks = len(bounds) - 1
        tiles, wide = nbx // 2, nbx // 4
        tall = cy + 16
        copies = 12 + 2 * chunks + chunks + nby - 1 + 4
        anywhere = pl.BlockSpec(memory_space=pl.ANY)
        V = pltpu.VMEM
        DMA = pltpu.SemaphoreType.DMA
        scratch = [
            V((6, 3, tall, nz), F32),
            V((3, cy + 8, nz), F32),
            V((cx, cy + 8, nz), F32),
            V((2, cx, cy + 8, nz), F32),
            V((2, cy, nz), F32),
            V((3, cx, cy, nz), F32),
            V((9, cy + 8, nz), F32),
            V((3, cy, nz), F32),
            V((3, cy, nz), F32),
            V((cx, cy, nz), F32),
            V((3, 3, tall, nz), F32),
            V((3, cx, cy, nz), F32),
            V((nbx, 128), jnp.int32),
            V((nbx, 128), jnp.int32),
            V((nbx, 128), jnp.int32),
            V((nbx, 128), F32),
            V((tiles, nz, 256), BF16),
            V((tiles, 1, 256), jnp.int32),
            V((wide, nz, 512), BF16),
            V((wide, 1, 512), jnp.int32),
            V((wide, rows, 512), BF16),
            V((2, 4 * rows, nz), BF16),
            V((2, cx, 3 * cy, nz), BF16),
            V((rows, nz), F32),
            V((cx, 3 * cy, nz), F32),
            V((nbx, 4, 128), F32),
            V((nbx, 4, 128), F32),
            V((nbx, 4, 128), F32),
            V((nbx, 4, 128), F32),
            V((8, nz), F32),
            V((8, 128), F32),
            V((nby - 1, 8, 128), F32),
            V((8, 128), F32),
            V((nbx, 8, 128), F32),
            DMA((7,)),
            DMA((7,)),
            DMA((copies,)),
            DMA((copies,)),
            DMA((nbx,)),
            DMA((nbx,)),
            DMA((nbx,)),
            DMA((nbx,)),
            DMA((nbx,)),
            DMA((nbx,)),
        ]
        flat = zone_mass.shape
        shapes = (displacement.shape, (3, 3, tall, nz), (2, cy, nz), (2, cy, nz))
        vel_x, mov_x, fin_x, old_x = pl.pallas_call(
            functools.partial(kernel, nbx, nby, cx, cy, nz, bounds),
            out_shape=tuple(jax.ShapeDtypeStruct(s, F32) for s in shapes),
            in_specs=[anywhere] * 7,
            out_specs=(anywhere,) * 4,
            scratch_shapes=scratch,
            compiler_params=pltpu.CompilerParams(
                collective_id=0, has_side_effects=True, vmem_limit_bytes=40 * 1024 * 1024
            ),
        )(displacement, velocity, zone_mass, energy, send_index, recv_index, contact_live)
        return pl.pallas_call(
            functools.partial(write_out, cy, nz),
            out_shape=tuple(
                jax.ShapeDtypeStruct(s, F32) for s in (displacement.shape, displacement.shape, flat, flat)
            ),
            in_specs=[anywhere] * 6,
            out_specs=(anywhere,) * 4,
            scratch_shapes=[
                V((3, cx, cy, nz), F32),
                V((3, 3, tall, nz), F32),
                V((2, cy, nz), F32),
                V((2, cy, nz), F32),
                V((cy, nz), F32),
                V((cy, nz), F32),
                V((2, cy, nz), F32),
                DMA((8,)),
                DMA((6,)),
            ],
            compiler_params=pltpu.CompilerParams(vmem_limit_bytes=16 * 1024 * 1024),
        )(vel_x, mov_x, fin_x, old_x, zone_mass, energy)

    field = P(None, "bx", "by", None)
    flat = P("bx", "by", None)
    panel = P("bx", "by", None, None)
    return jax.shard_map(
        local,
        mesh=mesh,
        in_specs=(field, field, flat, flat, panel, panel, panel),
        out_specs=(field, field, flat, flat),
        check_vma=False,
    )
```

```python
import functools

import jax
import jax.numpy as jnp
from jax import lax
from jax.experimental import pallas as pl
from jax.experimental.pallas import tpu as pltpu
from jax.sharding import PartitionSpec as P

MESH = pl.DeviceIdType.MESH
F32 = jnp.float32
BF16 = jnp.bfloat16


def split(x):
    hi = x.astype(BF16)
    lo = (x - hi.astype(F32)).astype(BF16)
    return hi, lo


def cross(a, b):
    return (
        a[1] * b[2] - a[2] * b[1],
        a[2] * b[0] - a[0] * b[2],
        a[0] * b[1] - a[1] * b[0],
    )


def dot3(a, b):
    return a[0] * b[0] + a[1] * b[1] + a[2] * b[2]


def roll_up(x):
    return pltpu.roll(x, x.shape[1] - 1, axis=1)


def roll_down(x):
    return pltpu.roll(x, 1, axis=1)


def edges(ref, field, plane, r):
    low = ref[field, plane, pl.ds(r, 16), :]
    high = ref[field, plane + 1, pl.ds(r, 16), :]
    l0, l1 = low[0:8], low[1:9]
    h0, h1 = high[0:8], high[1:9]
    lb, hb = l0 + l1, h0 + h1
    u1 = hb - lb
    u2 = (l1 - l0) + (h1 - h0)
    u3 = lb + hb
    return u1 + roll_up(u1), u2 + roll_up(u2), roll_up(u3) - u3


def geometry(ref, plane, r):
    parts = [edges(ref, f, plane, r) for f in range(3)]
    e1 = [parts[f][0] for f in range(3)]
    e2 = [parts[f][1] for f in range(3)]
    e3 = [parts[f][2] for f in range(3)]
    e1[0] = e1[0] + 4.0
    e2[1] = e2[1] + 4.0
    e3[2] = e3[2] + 4.0
    return e1, e2, e3


def finish(mov, plane, r, m, e, v0, stress):
    e1, e2, e3 = geometry(mov, plane, r)
    v = dot3(e1, cross(e2, e3)) * (1.0 / 64.0)
    rm = 1.0 / m
    return m / v, e - stress * (v - v0) * rm


def kernel(
    nbx, nby, cx, cy, nz, bounds,
    disp, vel, mass, ener, sidx, ridx, live,
    vel_x, mov_x, fin_x, old_x,
    nod, mas, ene, old, fin, frc, pan, fups, fupr, rmass, mov, velb,
    sids, rids, lives, wbuf,
    zm, mrow, zs, srow, rs, tab, taba, acce, accl,
    snd_e, rcv_e, snd_l, rcv_l, gmx, gms, gmr, gsx, gall,
    lsem, osem, ssem, rsem, ese, ere, esl, erl, esg, erg,
):
    X = lax.axis_index("bx")
    Y = lax.axis_index("by")
    xu, xd = lax.rem(X + 1, nbx), lax.rem(X + nbx - 1, nbx)
    yu, yd = lax.rem(Y + 1, nby), lax.rem(Y + nby - 1, nby)
    rows = cx * cy
    tiles = nbx // 2
    wide = nbx // 4
    chunks = len(bounds) - 1
    body = pl.ds(8, cy)

    barrier = pltpu.get_barrier_semaphore()
    for dev in ((xd, yd), (xd, yu), (xu, yd), (xu, yu)):
        pl.semaphore_signal(barrier, inc=1, device_id=dev, device_id_type=MESH)
    for d in range(1, nby):
        pl.semaphore_signal(barrier, inc=1, device_id=(X, lax.rem(Y + d, nby)), device_id_type=MESH)

    @pl.loop(1, nbx)
    def _(d):
        pl.semaphore_signal(barrier, inc=1, device_id=(lax.rem(X + d, nbx), Y), device_id_type=MESH)

    loads = [
        (sidx.at[0, 0], sids),
        (ridx.at[0, 0], rids),
        (live.at[0, 0], lives),
        (disp, nod.at[0:3, 0:2, body]),
        (vel, nod.at[3:6, 0:2, body]),
        (mass, mas.at[1:3, body]),
        (ener, ene.at[:, body]),
    ]
    loads = [pltpu.make_async_copy(s, d, lsem.at[i]) for i, (s, d) in enumerate(loads)]
    for c in loads:
        c.start()

    pl.semaphore_wait(barrier, 4 + nby - 1 + nbx - 1)

    def remote(src, dst, k, dev):
        return pltpu.make_async_remote_copy(
            src_ref=src, dst_ref=dst, send_sem=ssem.at[k], recv_sem=rsem.at[k],
            device_id=dev, device_id_type=MESH,
        )

    top, bottom = pl.ds(8 + cy, 8), pl.ds(0, 8)
    first, last = pl.ds(0, 8), pl.ds(cy - 8, 8)
    plan = [
        (mass.at[1], mas.at[0, body], (xu, Y)),
        (mass.at[1, last], mas.at[0, bottom], (xu, yu)),
        (mass.at[:, last], mas.at[1:3, bottom], (X, yu)),
        (ener.at[:, last], ene.at[:, bottom], (X, yu)),
        (disp.at[:, :, first], nod.at[0:3, 0:2, top], (X, yd)),
        (vel.at[:, :, first], nod.at[3:6, 0:2, top], (X, yd)),
        (disp.at[:, :, last], nod.at[0:3, 0:2, bottom], (X, yu)),
        (vel.at[:, :, last], nod.at[3:6, 0:2, bottom], (X, yu)),
        (disp.at[:, 0, last], nod.at[0:3, 2, bottom], (xd, yu)),
        (vel.at[:, 0, last], nod.at[3:6, 2, bottom], (xd, yu)),
        (disp.at[:, 0, first], nod.at[0:3, 2, top], (xd, yd)),
        (vel.at[:, 0, first], nod.at[3:6, 2, top], (xd, yd)),
    ]
    base = len(plan)
    for h in range(chunks):
        src, dst = pl.ds(bounds[h], bounds[h + 1] - bounds[h]), pl.ds(8 + bounds[h], bounds[h + 1] - bounds[h])
        plan.append((disp.at[:, 0, src], nod.at[0:3, 2, dst], (xd, Y)))
        plan.append((vel.at[:, 0, src], nod.at[3:6, 2, dst], (xd, Y)))
    halo = [remote(s, d, k, dev) for k, (s, d, dev) in enumerate(plan)]
    for c in halo:
        c.start()
    upk = len(plan)
    up = []
    edge = [0] + [b - 8 for b in bounds[1:-1]] + [cy]
    for h in range(chunks):
        cut = pl.ds(edge[h], edge[h + 1] - edge[h])
        up.append(remote(fups.at[:, cut], fupr.at[:, cut], upk + h, (xu, Y)))
    gmk = upk + chunks
    gm = [remote(gms, gmr.at[d - 1], gmk + d - 1, (X, lax.rem(Y + d, nby))) for d in range(1, nby)]
    lk = gmk + nby - 1
    late = [
        remote(mov.at[:, 0, body], mov.at[:, 2, body], lk, (xd, Y)),
        remote(mov.at[:, 0, pl.ds(8, 8)], mov.at[:, 2, top], lk + 1, (xd, yd)),
        remote(mov.at[:, 0, pl.ds(8, 8)], mov.at[:, 0, top], lk + 2, (X, yd)),
        remote(mov.at[:, 1, pl.ds(8, 8)], mov.at[:, 1, top], lk + 3, (X, yd)),
    ]

    def sending(snd, rcv, s_sem, r_sem, to, d):
        return pltpu.make_async_remote_copy(
            src_ref=snd, dst_ref=rcv.at[X], send_sem=s_sem.at[d], recv_sem=r_sem.at[d],
            device_id=(to, Y), device_id_type=MESH,
        )

    def arriving(snd, rcv, s_sem, r_sem, frm):
        d = lax.rem(X - frm + nbx, nbx)
        return pltpu.make_async_remote_copy(
            src_ref=snd, dst_ref=rcv.at[frm], send_sem=s_sem.at[d], recv_sem=r_sem.at[d],
            device_id=(frm, Y), device_id_type=MESH,
        )

    for c in loads[:3]:
        c.wait()
    shift = nz.bit_length() - 1

    def line_up(ref, t, count):
        return jnp.concatenate([ref[pl.ds(count * t + i, 1), :] for i in range(count)], axis=1)

    def hot(length, index):
        line = lax.broadcasted_iota(jnp.int32, (length, index.shape[1]), 0)
        return jnp.where(line == index, 1.0, 0.0).astype(BF16)

    @pl.loop(0, tiles)
    def _(t):
        idx = line_up(sids, t, 2)
        mrow[t] = lax.shift_right_logical(idx, shift)
        zm[t] = hot(nz, jnp.bitwise_and(idx, nz - 1))

    @pl.loop(0, wide)
    def _(t):
        idx = line_up(rids, t, 4)
        row = lax.shift_right_logical(idx, shift)
        srow[t] = row
        zs[t] = hot(nz, jnp.bitwise_and(idx, nz - 1))
        rs[t] = hot(rows, row)

    def zone(z, r, carry):
        e1, e2, e3 = geometry(nod, z, r)
        grads = [edges(nod, 3 + f, z, r) for f in range(3)]
        g1 = [g[0] for g in grads]
        g2 = [g[1] for g in grads]
        g3 = [g[2] for g in grads]
        a1, a2, a3 = cross(e2, e3), cross(e3, e1), cross(e1, e2)
        v = dot3(e1, a1) * (1.0 / 64.0)
        rate = (dot3(g1, a1) + dot3(g2, a2) + dot3(g3, a3)) * (1.0 / 64.0)
        m = mas[z + 1, pl.ds(r, 8), :]
        e = ene[z, pl.ds(r, 8), :]
        rv = 1.0 / v
        rho = m * rv
        cs = jnp.sqrt(0.56 * e)
        length = jnp.exp(jnp.log(v) * (1.0 / 3.0))
        length = length + length * (v - length * length * length) * rv * (1.0 / 3.0)
        ld = length * jnp.minimum(rate * rv, 0.0)
        stress = rho * (0.4 * e + ld * (ld - 0.25 * cs))
        peak = jnp.abs(g1[0])
        for g in g1[1:] + g2 + g3:
            peak = jnp.maximum(peak, jnp.abs(g))
        inverse = cs * length * length * rv + peak
        k = stress * (1.0 / 64.0)
        old[0, z, pl.ds(r, 8), :] = v
        old[1, z, pl.ds(r, 8), :] = stress
        for f in range(3):
            p1, p2, p3 = k * a1[f], k * a2[f], k * a3[f]
            q1 = p1 + roll_down(p1)
            q2 = p2 + roll_down(p2)
            q3 = roll_down(p3) - p3
            pan[f, pl.ds(r, 8), :] = q3 - q1
            pan[3 + f, pl.ds(r, 8), :] = q3 + q1
            pan[6 + f, pl.ds(r, 8), :] = q2
        return jnp.maximum(carry, inverse)

    def force(z, r):
        for f in range(3):
            qm = pan[f, pl.ds(r - 8, 16), :]
            qp = pan[3 + f, pl.ds(r - 8, 16), :]
            q2 = pan[6 + f, pl.ds(r - 8, 16), :]
            here = slice(8, 16)
            back = slice(7, 15)
            turn = q2[back] - q2[here]
            lower = qm[here] + qm[back] + turn
            upper = qp[here] + qp[back] + turn
            at = pl.ds(r - 8, 8)
            if z == 0:
                frc[f, 0, at, :] = lower
                frc[f, 1, at, :] = upper
            else:
                frc[f, 1, at, :] = frc[f, 1, at, :] + lower
                fups[f, at, :] = upper

    def zones(z, lo, hi):
        def step(i, carry):
            r = pl.multiple_of(i * 8, 8)
            carry = zone(z, r, carry)

            @pl.when(i > 0)
            def _():
                force(z, r)
            return carry
        gmx[...] = lax.fori_loop(lo, hi, step, gmx[...])

    gmx[...] = jnp.zeros_like(gmx)
    for c in loads[3:]:
        c.wait()
    for c in halo[2:8]:
        c.wait()
    zones(0, 0, cy // 8 + 1)

    for c in halo[0:2]:
        c.wait()

    @pl.loop(0, cy // 16)
    def _(i):
        b = pl.multiple_of(i * 16, 16)
        s = [mas[p, pl.ds(b, 24), :] for p in range(3)]
        for p in range(2):
            t = s[p] + s[p + 1]
            t = t[8:24] + t[7:23]
            m = 0.125 * (t + roll_down(t))
            rmass[p, pl.ds(b, 16), :] = 1.0 / m
            at = pl.multiple_of(p * cy + b, 16)
            for f in range(4):
                hi, lo = split(m if f == 3 else nod[3 + f, p, pl.ds(8 + b, 16), :])
                tab[0, pl.ds(f * rows + at, 16), :] = hi
                tab[1, pl.ds(f * rows + at, 16), :] = lo

    def gather(high, low, z, row, length):
        o = jnp.dot(high, z, preferred_element_type=F32)
        o = o + jnp.dot(low, z, preferred_element_type=F32)
        hit = lax.broadcasted_iota(jnp.int32, (length, z.shape[1]), 0) == row
        return [
            jnp.sum(jnp.where(hit, o[b : b + length], 0.0), axis=0, keepdims=True)
            for b in range(0, o.shape[0], length)
        ]

    @pl.loop(0, tiles)
    def _(t):
        for f, g in enumerate(gather(tab[0], tab[1], zm[t], mrow[t], rows)):
            snd_e[2 * t, f : f + 1, :] = g[:, :128]
            snd_e[2 * t + 1, f : f + 1, :] = g[:, 128:]

    @pl.loop(1, nbx)
    def _(d):
        to = lax.rem(X + d, nbx)
        sending(snd_e.at[to], rcv_e, ese, ere, to, d).start()
    rcv_e[X] = snd_e[X]

    def chunk_zones(h):
        halo[base + 2 * h].wait()
        halo[base + 2 * h + 1].wait()
        if h == 0:
            for c in halo[8:10]:
                c.wait()
        if h == chunks - 1:
            for c in halo[10:12]:
                c.wait()
        lo = 0 if h == 0 else bounds[h] // 8
        hi = cy // 8 + 1 if h == chunks - 1 else bounds[h + 1] // 8
        zones(1, lo, hi)
        up[h].start()

    for h in range(chunks - 1):
        chunk_zones(h)

    cut = pl.ds(3 * rows, rows)

    @pl.loop(0, wide)
    def _(t):
        (g,) = gather(tab[0, cut, :], tab[1, cut, :], zs[t], srow[t], rows)
        for i in range(4):
            wbuf[pl.ds(4 * t + i, 1), :] = g[:, 128 * i : 128 * i + 128]

    @pl.loop(1, nbx)
    def _(d):
        to = lax.rem(X + d, nbx)
        sending(snd_e.at[to], rcv_e, ese, ere, to, d).wait_send()
        frm = lax.rem(X + nbx - d, nbx)
        arriving(snd_e.at[frm], rcv_e, ese, ere, frm).wait_recv()

    @pl.loop(0, nbx)
    def _(s):
        mm = rcv_e[s, 3:4, :]
        ms = wbuf[pl.ds(s, 1), :]
        wbuf[pl.ds(s, 1), :] = lives[pl.ds(s, 1), :].astype(F32) * 0.5 * mm / (mm + ms)

    chunk_zones(chunks - 1)

    peak = gmx[:, :128]
    for b in range(128, nz, 128):
        peak = jnp.maximum(peak, gmx[:, b : b + 128])
    gms[...] = peak
    for c in gm:
        c.start()

    def accel(p):
        @pl.loop(0, cy // 16)
        def _(i):
            b = pl.multiple_of(i * 16, 16)
            rm = rmass[p, pl.ds(b, 16), :]
            for f in range(3):
                a = frc[f, p, pl.ds(b, 16), :]
                if p == 0:
                    a = a + fupr[f, pl.ds(b, 16), :]
                a = a * rm
                frc[f, p, pl.ds(b, 16), :] = a
                hi, lo = split(a)
                at = pl.ds(pl.multiple_of(f * cy + b, 16), 16)
                taba[0, p, at, :] = hi
                taba[1, p, at, :] = lo

    accel(1)

    def scatter(acc, rhs, hits, values):
        parts = ([], [])
        for v in values:
            for side, piece in zip(parts, split(v)):
                side.append(hits * piece)
        o = acc[...]
        for side in parts:
            lhs = side[0] if len(side) == 1 else jnp.concatenate(side, axis=0)
            o = o + lax.dot_general(lhs, rhs, (((1,), (1,)), ((), ())), preferred_element_type=F32)
        acc[...] = o

    acce[...] = jnp.zeros_like(acce)

    @pl.loop(0, wide)
    def _(t):
        scatter(acce, zs[t], rs[t], [line_up(wbuf, t, 4)])

    for c in gm:
        c.wait()
    g = gms[...]
    for d in range(1, nby):
        g = jnp.maximum(g, gmr[d - 1])
    gsx[...] = g
    gall[X] = g

    @pl.loop(1, nbx)
    def _(d):
        sending(gsx, gall, esg, erg, lax.rem(X + d, nbx), d).start()

    @pl.loop(0, tiles)
    def _(t):
        for f, g in enumerate(gather(taba[0, 1], taba[1, 1], zm[t], mrow[t] - cy, cy)):
            snd_l[2 * t, f : f + 1, :] = g[:, :128]
            snd_l[2 * t + 1, f : f + 1, :] = g[:, 128:]

    for c in up:
        c.wait()
    accel(0)
    mine = X // 2

    @pl.loop(0, tiles)
    def _(i):
        t = lax.rem(i + mine, tiles)
        for f, g in enumerate(gather(taba[0, 0], taba[1, 0], zm[t], mrow[t], cy)):
            snd_l[2 * t, f : f + 1, :] = snd_l[2 * t, f : f + 1, :] + g[:, :128]
            snd_l[2 * t + 1, f : f + 1, :] = snd_l[2 * t + 1, f : f + 1, :] + g[:, 128:]
        for k in range(2):
            to = 2 * t + k

            @pl.when(to != X)
            def _():
                sending(snd_l.at[to], rcv_l, esl, erl, to, lax.rem(to - X + nbx, nbx)).start()
    rcv_l[X] = snd_l[X]

    @pl.loop(1, nbx)
    def _(d):
        sending(gsx, gall, esg, erg, lax.rem(X + d, nbx), d).wait_send()
        arriving(gsx, gall, esg, erg, lax.rem(X + nbx - d, nbx)).wait_recv()
    g = lax.fori_loop(1, nbx, lambda d, c: jnp.maximum(c, gall[d]), gall[0])
    g = jnp.max(jnp.max(g, axis=0, keepdims=True), axis=1, keepdims=True)
    dt = 0.25 / jnp.broadcast_to(g, (8, nz))
    dt_row = dt[0:1, 0:128]

    accl[...] = jnp.zeros_like(accl)

    def late_scatter(p):
        @pl.loop(0, wide)
        def _(i):
            t = lax.rem(X // 4 - i + wide, wide)
            if p == 0:
                for k in range(4):
                    frm = 4 * t + k

                    @pl.when(frm != X)
                    def _():
                        arriving(snd_l.at[frm], rcv_l, esl, erl, frm).wait_recv()
            w = line_up(wbuf, t, 4)
            values = []
            for f in range(3):
                moved = [
                    rcv_e[4 * t + k, f : f + 1, :] + dt_row * rcv_l[4 * t + k, f : f + 1, :]
                    for k in range(4)
                ]
                values.append(w * jnp.concatenate(moved, axis=1))
            scatter(accl.at[p], zs[t], rs[t, p * cy : (p + 1) * cy, :], values)

    def move(p):
        @pl.loop(0, cy // 8)
        def _(i):
            b = pl.multiple_of(i * 8, 8)
            at = pl.multiple_of(p * cy + b, 8)
            keep = 1.0 - acce[pl.ds(at, 8), :]
            for f in range(3):
                v = nod[3 + f, p, pl.ds(8 + b, 8), :] + dt * frc[f, p, pl.ds(b, 8), :]
                v = v * keep + accl[p, pl.ds(pl.multiple_of(f * cy + b, 8), 8), :]
                velb[f, p, pl.ds(b, 8), :] = v
                mov[f, p, pl.ds(8 + b, 8), :] = nod[f, p, pl.ds(8 + b, 8), :] + dt * v

    late_scatter(0)
    move(0)
    for c in late[:3]:
        c.start()
    late_scatter(1)
    move(1)
    late[3].start()
    outs = [
        pltpu.make_async_copy(velb, vel_x, osem.at[0]),
        pltpu.make_async_copy(old.at[:, 1, body], old_x, osem.at[1]),
        pltpu.make_async_copy(mov.at[:, 0, body], mov_x.at[:, 0, body], osem.at[2]),
        pltpu.make_async_copy(mov.at[:, 1, body], mov_x.at[:, 1, body], osem.at[3]),
    ]
    for c in outs:
        c.start()

    @pl.loop(1, nbx)
    def _(d):
        to = lax.rem(X + d, nbx)
        sending(snd_l.at[to], rcv_l, esl, erl, to, d).wait_send()

    late[2].wait()
    late[3].wait()

    @pl.loop(0, cy // 8)
    def _(i):
        b = pl.multiple_of(i * 8, 8)
        r = pl.multiple_of(8 + b, 8)
        at = pl.ds(r, 8)
        d, e = finish(mov, 0, r, mas[1, at, :], ene[0, at, :], old[0, 0, at, :], old[1, 0, at, :])
        fin[0, pl.ds(b, 8), :] = d
        fin[1, pl.ds(b, 8), :] = e
    ends = [
        pltpu.make_async_copy(fin, fin_x, osem.at[4]),
        pltpu.make_async_copy(mov.at[:, 1, top], mov_x.at[:, 1, top], osem.at[5]),
        pltpu.make_async_copy(mov.at[:, 2, pl.ds(8, cy + 8)], mov_x.at[:, 2, pl.ds(8, cy + 8)], osem.at[6]),
    ]
    ends[0].start()
    ends[1].start()
    late[0].wait()
    late[1].wait()
    ends[2].start()
    for c in outs + ends:
        c.wait()


def write_out(
    cy, nz, vel_x, mov_x, fin_x, old_x, mass, ener, vel_o, disp_o, den_o, ene_o,
    velb, mov, fin, old, mas, ene, res, isem, osem,
):
    body = pl.ds(8, cy)
    ins = [
        (mov_x.at[:, 1, pl.ds(8, cy + 8)], mov.at[:, 1, pl.ds(8, cy + 8)]),
        (mov_x.at[:, 2, pl.ds(8, cy + 8)], mov.at[:, 2, pl.ds(8, cy + 8)]),
        (old_x, old),
        (mass.at[1], mas),
        (ener.at[1], ene),
        (mov_x.at[:, 0, body], mov.at[:, 0, body]),
        (vel_x, velb),
        (fin_x, fin),
    ]
    ins = [pltpu.make_async_copy(s, d, isem.at[i]) for i, (s, d) in enumerate(ins)]
    for c in ins:
        c.start()
    for c in ins[:5]:
        c.wait()

    def step(i, _):
        b = pl.multiple_of(i * 8, 8)
        at = pl.ds(b, 8)
        d, e = finish(
            mov, 1, pl.multiple_of(8 + b, 8), mas[at, :], ene[at, :], old[0, at, :], old[1, at, :]
        )
        res[0, at, :] = d
        res[1, at, :] = e
        return 0

    half = cy // 16
    lax.fori_loop(0, half, step, 0)
    for c in ins[5:]:
        c.wait()
    outs = [
        (velb, vel_o),
        (mov.at[:, 0:2, body], disp_o),
        (fin.at[0], den_o.at[0]),
        (fin.at[1], ene_o.at[0]),
        (res.at[0], den_o.at[1]),
        (res.at[1], ene_o.at[1]),
    ]
    outs = [pltpu.make_async_copy(s, d, osem.at[i]) for i, (s, d) in enumerate(outs)]
    for c in outs[:4]:
        c.start()
    lax.fori_loop(half, cy // 8, step, 0)
    for c in outs[4:]:
        c.start()
    for c in outs:
        c.wait()


def solution(mesh):
    nbx, nby = mesh.shape["bx"], mesh.shape["by"]

    def local(displacement, velocity, zone_mass, energy, send_index, recv_index, contact_live):
        _, cx, cy, nz = displacement.shape
        displacement, velocity, zone_mass, energy, send_index, recv_index, contact_live = [
            pltpu.with_memory_space_constraint(x, pltpu.HBM)
            for x in (displacement, velocity, zone_mass, energy, send_index, recv_index, contact_live)
        ]
        rows = cx * cy
        bounds = (0, 48, 88, 112, 128) if cy == 128 else (0, cy // 2, cy)
        chunks = len(bounds) - 1
        tiles, wide = nbx // 2, nbx // 4
        tall = cy + 16
        copies = 12 + 2 * chunks + chunks + nby - 1 + 4
        anywhere = pl.BlockSpec(memory_space=pl.ANY)
        V = pltpu.VMEM
        DMA = pltpu.SemaphoreType.DMA
        scratch = [
            V((6, 3, tall, nz), F32),
            V((3, cy + 8, nz), F32),
            V((cx, cy + 8, nz), F32),
            V((2, cx, cy + 8, nz), F32),
            V((2, cy, nz), F32),
            V((3, cx, cy, nz), F32),
            V((9, cy + 8, nz), F32),
            V((3, cy, nz), F32),
            V((3, cy, nz), F32),
            V((cx, cy, nz), F32),
            V((3, 3, tall, nz), F32),
            V((3, cx, cy, nz), F32),
            V((nbx, 128), jnp.int32),
            V((nbx, 128), jnp.int32),
            V((nbx, 128), jnp.int32),
            V((nbx, 128), F32),
            V((tiles, nz, 256), BF16),
            V((tiles, 1, 256), jnp.int32),
            V((wide, nz, 512), BF16),
            V((wide, 1, 512), jnp.int32),
            V((wide, rows, 512), BF16),
            V((2, 4 * rows, nz), BF16),
            V((2, cx, 3 * cy, nz), BF16),
            V((rows, nz), F32),
            V((cx, 3 * cy, nz), F32),
            V((nbx, 4, 128), F32),
            V((nbx, 4, 128), F32),
            V((nbx, 4, 128), F32),
            V((nbx, 4, 128), F32),
            V((8, nz), F32),
            V((8, 128), F32),
            V((nby - 1, 8, 128), F32),
            V((8, 128), F32),
            V((nbx, 8, 128), F32),
            DMA((7,)),
            DMA((7,)),
            DMA((copies,)),
            DMA((copies,)),
            DMA((nbx,)),
            DMA((nbx,)),
            DMA((nbx,)),
            DMA((nbx,)),
            DMA((nbx,)),
            DMA((nbx,)),
        ]
        flat = zone_mass.shape
        shapes = (displacement.shape, (3, 3, tall, nz), (2, cy, nz), (2, cy, nz))
        vel_x, mov_x, fin_x, old_x = pl.pallas_call(
            functools.partial(kernel, nbx, nby, cx, cy, nz, bounds),
            out_shape=tuple(jax.ShapeDtypeStruct(s, F32) for s in shapes),
            in_specs=[anywhere] * 7,
            out_specs=(anywhere,) * 4,
            scratch_shapes=scratch,
            compiler_params=pltpu.CompilerParams(
                collective_id=0, has_side_effects=True, vmem_limit_bytes=40 * 1024 * 1024
            ),
        )(displacement, velocity, zone_mass, energy, send_index, recv_index, contact_live)
        return pl.pallas_call(
            functools.partial(write_out, cy, nz),
            out_shape=tuple(
                jax.ShapeDtypeStruct(s, F32) for s in (displacement.shape, displacement.shape, flat, flat)
            ),
            in_specs=[anywhere] * 6,
            out_specs=(anywhere,) * 4,
            scratch_shapes=[
                V((3, cx, cy, nz), F32),
                V((3, 3, tall, nz), F32),
                V((2, cy, nz), F32),
                V((2, cy, nz), F32),
                V((cy, nz), F32),
                V((cy, nz), F32),
                V((2, cy, nz), F32),
                DMA((8,)),
                DMA((6,)),
            ],
            compiler_params=pltpu.CompilerParams(vmem_limit_bytes=16 * 1024 * 1024),
        )(vel_x, mov_x, fin_x, old_x, zone_mass, energy)

    field = P(None, "bx", "by", None)
    flat = P("bx", "by", None)
    panel = P("bx", "by", None, None)
    return jax.shard_map(
        local,
        mesh=mesh,
        in_specs=(field, field, flat, flat, panel, panel, panel),
        out_specs=(field, field, flat, flat),
        check_vma=False,
    )
```

```python
import functools

import jax
import jax.numpy as jnp
from jax import lax
from jax.experimental import pallas as pl
from jax.experimental.pallas import tpu as pltpu
from jax.sharding import PartitionSpec as P

MESH = pl.DeviceIdType.MESH
F32 = jnp.float32
BF16 = jnp.bfloat16


def split(x):
    hi = x.astype(BF16)
    lo = (x - hi.astype(F32)).astype(BF16)
    return hi, lo


def cross(a, b):
    return (
        a[1] * b[2] - a[2] * b[1],
        a[2] * b[0] - a[0] * b[2],
        a[0] * b[1] - a[1] * b[0],
    )


def dot3(a, b):
    return a[0] * b[0] + a[1] * b[1] + a[2] * b[2]


def roll_up(x):
    return pltpu.roll(x, x.shape[1] - 1, axis=1)


def roll_down(x):
    return pltpu.roll(x, 1, axis=1)


def edges(ref, field, plane, r):
    low = ref[field, plane, pl.ds(r, 16), :]
    high = ref[field, plane + 1, pl.ds(r, 16), :]
    l0, l1 = low[0:8], low[1:9]
    h0, h1 = high[0:8], high[1:9]
    lb, hb = l0 + l1, h0 + h1
    u1 = hb - lb
    u2 = (l1 - l0) + (h1 - h0)
    u3 = lb + hb
    return u1 + roll_up(u1), u2 + roll_up(u2), roll_up(u3) - u3


def geometry(ref, plane, r):
    parts = [edges(ref, f, plane, r) for f in range(3)]
    e1 = [parts[f][0] for f in range(3)]
    e2 = [parts[f][1] for f in range(3)]
    e3 = [parts[f][2] for f in range(3)]
    e1[0] = e1[0] + 4.0
    e2[1] = e2[1] + 4.0
    e3[2] = e3[2] + 4.0
    return e1, e2, e3


def finish(mov, plane, r, m, e, v0, stress):
    e1, e2, e3 = geometry(mov, plane, r)
    v = dot3(e1, cross(e2, e3)) * (1.0 / 64.0)
    rm = 1.0 / m
    return m / v, e - stress * (v - v0) * rm


def kernel(
    nbx, nby, cx, cy, nz, bounds,
    disp, vel, mass, ener, sidx, ridx, live,
    vel_x, mov_x, fin_x, old_x,
    nod, mas, ene, old, fin, frc, pan, fups, fupr, rmass, mov, velb,
    sids, rids, lives, wbuf,
    zm, mrow, zs, srow, rs, tab, taba, acce, accl,
    snd_e, rcv_e, snd_l, rcv_l, gmx, gms, gmr, gsx, gall,
    lsem, osem, ssem, rsem, ese, ere, esl, erl, esg, erg,
):
    X = lax.axis_index("bx")
    Y = lax.axis_index("by")
    xu, xd = lax.rem(X + 1, nbx), lax.rem(X + nbx - 1, nbx)
    yu, yd = lax.rem(Y + 1, nby), lax.rem(Y + nby - 1, nby)
    rows = cx * cy
    tiles = nbx // 2
    wide = nbx // 4
    chunks = len(bounds) - 1
    body = pl.ds(8, cy)

    barrier = pltpu.get_barrier_semaphore()
    for dev in ((xd, yd), (xd, yu), (xu, yd), (xu, yu)):
        pl.semaphore_signal(barrier, inc=1, device_id=dev, device_id_type=MESH)
    for d in range(1, nby):
        pl.semaphore_signal(barrier, inc=1, device_id=(X, lax.rem(Y + d, nby)), device_id_type=MESH)

    @pl.loop(1, nbx)
    def _(d):
        pl.semaphore_signal(barrier, inc=1, device_id=(lax.rem(X + d, nbx), Y), device_id_type=MESH)

    loads = [
        (sidx.at[0, 0], sids),
        (ridx.at[0, 0], rids),
        (live.at[0, 0], lives),
        (disp, nod.at[0:3, 0:2, body]),
        (vel, nod.at[3:6, 0:2, body]),
        (mass, mas.at[1:3, body]),
        (ener, ene.at[:, body]),
    ]
    loads = [pltpu.make_async_copy(s, d, lsem.at[i]) for i, (s, d) in enumerate(loads)]
    for c in loads:
        c.start()

    pl.semaphore_wait(barrier, 4 + nby - 1 + nbx - 1)

    def remote(src, dst, k, dev):
        return pltpu.make_async_remote_copy(
            src_ref=src, dst_ref=dst, send_sem=ssem.at[k], recv_sem=rsem.at[k],
            device_id=dev, device_id_type=MESH,
        )

    top, bottom = pl.ds(8 + cy, 8), pl.ds(0, 8)
    first, last = pl.ds(0, 8), pl.ds(cy - 8, 8)
    plan = [
        (mass.at[1], mas.at[0, body], (xu, Y)),
        (mass.at[1, last], mas.at[0, bottom], (xu, yu)),
        (mass.at[:, last], mas.at[1:3, bottom], (X, yu)),
        (ener.at[:, last], ene.at[:, bottom], (X, yu)),
        (disp.at[:, :, first], nod.at[0:3, 0:2, top], (X, yd)),
        (vel.at[:, :, first], nod.at[3:6, 0:2, top], (X, yd)),
        (disp.at[:, :, last], nod.at[0:3, 0:2, bottom], (X, yu)),
        (vel.at[:, :, last], nod.at[3:6, 0:2, bottom], (X, yu)),
        (disp.at[:, 0, last], nod.at[0:3, 2, bottom], (xd, yu)),
        (vel.at[:, 0, last], nod.at[3:6, 2, bottom], (xd, yu)),
        (disp.at[:, 0, first], nod.at[0:3, 2, top], (xd, yd)),
        (vel.at[:, 0, first], nod.at[3:6, 2, top], (xd, yd)),
    ]
    base = len(plan)
    for h in range(chunks):
        src, dst = pl.ds(bounds[h], bounds[h + 1] - bounds[h]), pl.ds(8 + bounds[h], bounds[h + 1] - bounds[h])
        plan.append((disp.at[:, 0, src], nod.at[0:3, 2, dst], (xd, Y)))
        plan.append((vel.at[:, 0, src], nod.at[3:6, 2, dst], (xd, Y)))
    halo = [remote(s, d, k, dev) for k, (s, d, dev) in enumerate(plan)]
    for c in halo:
        c.start()
    upk = len(plan)
    up = []
    edge = [0] + [b - 8 for b in bounds[1:-1]] + [cy]
    for h in range(chunks):
        cut = pl.ds(edge[h], edge[h + 1] - edge[h])
        up.append(remote(fups.at[:, cut], fupr.at[:, cut], upk + h, (xu, Y)))
    gmk = upk + chunks
    gm = [remote(gms, gmr.at[d - 1], gmk + d - 1, (X, lax.rem(Y + d, nby))) for d in range(1, nby)]
    lk = gmk + nby - 1
    late = [
        remote(mov.at[:, 0, body], mov_x.at[:, 2, body], lk, (xd, Y)),
        remote(mov.at[:, 0, pl.ds(8, 8)], mov_x.at[:, 2, top], lk + 1, (xd, yd)),
        remote(mov.at[:, 0, pl.ds(8, 8)], mov.at[:, 0, top], lk + 2, (X, yd)),
        remote(mov.at[:, 1, pl.ds(8, 8)], mov.at[:, 1, top], lk + 3, (X, yd)),
    ]

    def sending(snd, rcv, s_sem, r_sem, to, d):
        return pltpu.make_async_remote_copy(
            src_ref=snd, dst_ref=rcv.at[X], send_sem=s_sem.at[d], recv_sem=r_sem.at[d],
            device_id=(to, Y), device_id_type=MESH,
        )

    def arriving(snd, rcv, s_sem, r_sem, frm):
        d = lax.rem(X - frm + nbx, nbx)
        return pltpu.make_async_remote_copy(
            src_ref=snd, dst_ref=rcv.at[frm], send_sem=s_sem.at[d], recv_sem=r_sem.at[d],
            device_id=(frm, Y), device_id_type=MESH,
        )

    for c in loads[:3]:
        c.wait()
    shift = nz.bit_length() - 1

    def line_up(ref, t, count):
        return jnp.concatenate([ref[pl.ds(count * t + i, 1), :] for i in range(count)], axis=1)

    def hot(length, index):
        line = lax.broadcasted_iota(jnp.int32, (length, index.shape[1]), 0)
        return jnp.where(line == index, 1.0, 0.0).astype(BF16)

    @pl.loop(0, tiles)
    def _(t):
        idx = line_up(sids, t, 2)
        mrow[t] = lax.shift_right_logical(idx, shift)
        zm[t] = hot(nz, jnp.bitwise_and(idx, nz - 1))

    @pl.loop(0, wide)
    def _(t):
        idx = line_up(rids, t, 4)
        row = lax.shift_right_logical(idx, shift)
        srow[t] = row
        zs[t] = hot(nz, jnp.bitwise_and(idx, nz - 1))
        rs[t] = hot(rows, row)

    def zone(z, r, carry):
        e1, e2, e3 = geometry(nod, z, r)
        grads = [edges(nod, 3 + f, z, r) for f in range(3)]
        g1 = [g[0] for g in grads]
        g2 = [g[1] for g in grads]
        g3 = [g[2] for g in grads]
        a1, a2, a3 = cross(e2, e3), cross(e3, e1), cross(e1, e2)
        v = dot3(e1, a1) * (1.0 / 64.0)
        rate = (dot3(g1, a1) + dot3(g2, a2) + dot3(g3, a3)) * (1.0 / 64.0)
        m = mas[z + 1, pl.ds(r, 8), :]
        e = ene[z, pl.ds(r, 8), :]
        rv = 1.0 / v
        rho = m * rv
        cs = jnp.sqrt(0.56 * e)
        length = jnp.exp(jnp.log(v) * (1.0 / 3.0))
        length = length + length * (v - length * length * length) * rv * (1.0 / 3.0)
        ld = length * jnp.minimum(rate * rv, 0.0)
        stress = rho * (0.4 * e + ld * (ld - 0.25 * cs))
        peak = jnp.abs(g1[0])
        for g in g1[1:] + g2 + g3:
            peak = jnp.maximum(peak, jnp.abs(g))
        inverse = cs * length * length * rv + peak
        k = stress * (1.0 / 64.0)
        old[0, z, pl.ds(r, 8), :] = v
        old[1, z, pl.ds(r, 8), :] = stress
        for f in range(3):
            p1, p2, p3 = k * a1[f], k * a2[f], k * a3[f]
            q1 = p1 + roll_down(p1)
            q2 = p2 + roll_down(p2)
            q3 = roll_down(p3) - p3
            pan[f, pl.ds(r, 8), :] = q3 - q1
            pan[3 + f, pl.ds(r, 8), :] = q3 + q1
            pan[6 + f, pl.ds(r, 8), :] = q2
        return jnp.maximum(carry, inverse)

    def force(z, r):
        for f in range(3):
            qm = pan[f, pl.ds(r - 8, 16), :]
            qp = pan[3 + f, pl.ds(r - 8, 16), :]
            q2 = pan[6 + f, pl.ds(r - 8, 16), :]
            here = slice(8, 16)
            back = slice(7, 15)
            turn = q2[back] - q2[here]
            lower = qm[here] + qm[back] + turn
            upper = qp[here] + qp[back] + turn
            at = pl.ds(r - 8, 8)
            if z == 0:
                frc[f, 0, at, :] = lower
                frc[f, 1, at, :] = upper
            else:
                frc[f, 1, at, :] = frc[f, 1, at, :] + lower
                fups[f, at, :] = upper

    def zones(z, lo, hi):
        def step(i, carry):
            r = pl.multiple_of(i * 8, 8)
            carry = zone(z, r, carry)

            @pl.when(i > 0)
            def _():
                force(z, r)
            return carry
        gmx[...] = lax.fori_loop(lo, hi, step, gmx[...])

    gmx[...] = jnp.zeros_like(gmx)
    for c in loads[3:]:
        c.wait()
    for c in halo[2:8]:
        c.wait()
    zones(0, 0, cy // 8 + 1)

    for c in halo[0:2]:
        c.wait()

    @pl.loop(0, cy // 16)
    def _(i):
        b = pl.multiple_of(i * 16, 16)
        s = [mas[p, pl.ds(b, 24), :] for p in range(3)]
        for p in range(2):
            t = s[p] + s[p + 1]
            t = t[8:24] + t[7:23]
            m = 0.125 * (t + roll_down(t))
            rmass[p, pl.ds(b, 16), :] = 1.0 / m
            at = pl.multiple_of(p * cy + b, 16)
            for f in range(4):
                hi, lo = split(m if f == 3 else nod[3 + f, p, pl.ds(8 + b, 16), :])
                tab[0, pl.ds(f * rows + at, 16), :] = hi
                tab[1, pl.ds(f * rows + at, 16), :] = lo

    def gather(high, low, z, row, length):
        o = jnp.dot(high, z, preferred_element_type=F32)
        o = o + jnp.dot(low, z, preferred_element_type=F32)
        hit = lax.broadcasted_iota(jnp.int32, (length, z.shape[1]), 0) == row
        return [
            jnp.sum(jnp.where(hit, o[b : b + length], 0.0), axis=0, keepdims=True)
            for b in range(0, o.shape[0], length)
        ]

    @pl.loop(0, tiles)
    def _(t):
        for f, g in enumerate(gather(tab[0], tab[1], zm[t], mrow[t], rows)):
            snd_e[2 * t, f : f + 1, :] = g[:, :128]
            snd_e[2 * t + 1, f : f + 1, :] = g[:, 128:]

    @pl.loop(1, nbx)
    def _(d):
        to = lax.rem(X + d, nbx)
        sending(snd_e.at[to], rcv_e, ese, ere, to, d).start()
    rcv_e[X] = snd_e[X]

    def chunk_zones(h):
        halo[base + 2 * h].wait()
        halo[base + 2 * h + 1].wait()
        if h == 0:
            for c in halo[8:10]:
                c.wait()
        if h == chunks - 1:
            for c in halo[10:12]:
                c.wait()
        lo = 0 if h == 0 else bounds[h] // 8
        hi = cy // 8 + 1 if h == chunks - 1 else bounds[h + 1] // 8
        zones(1, lo, hi)
        up[h].start()

    for h in range(chunks - 1):
        chunk_zones(h)

    cut = pl.ds(3 * rows, rows)

    @pl.loop(0, wide)
    def _(t):
        (g,) = gather(tab[0, cut, :], tab[1, cut, :], zs[t], srow[t], rows)
        for i in range(4):
            wbuf[pl.ds(4 * t + i, 1), :] = g[:, 128 * i : 128 * i + 128]

    @pl.loop(1, nbx)
    def _(d):
        to = lax.rem(X + d, nbx)
        sending(snd_e.at[to], rcv_e, ese, ere, to, d).wait_send()
        frm = lax.rem(X + nbx - d, nbx)
        arriving(snd_e.at[frm], rcv_e, ese, ere, frm).wait_recv()

    @pl.loop(0, nbx)
    def _(s):
        mm = rcv_e[s, 3:4, :]
        ms = wbuf[pl.ds(s, 1), :]
        wbuf[pl.ds(s, 1), :] = lives[pl.ds(s, 1), :].astype(F32) * 0.5 * mm / (mm + ms)

    chunk_zones(chunks - 1)

    peak = gmx[:, :128]
    for b in range(128, nz, 128):
        peak = jnp.maximum(peak, gmx[:, b : b + 128])
    gms[...] = peak
    for c in gm:
        c.start()

    def accel(p):
        @pl.loop(0, cy // 16)
        def _(i):
            b = pl.multiple_of(i * 16, 16)
            rm = rmass[p, pl.ds(b, 16), :]
            for f in range(3):
                a = frc[f, p, pl.ds(b, 16), :]
                if p == 0:
                    a = a + fupr[f, pl.ds(b, 16), :]
                a = a * rm
                frc[f, p, pl.ds(b, 16), :] = a
                hi, lo = split(a)
                at = pl.ds(pl.multiple_of(f * cy + b, 16), 16)
                taba[0, p, at, :] = hi
                taba[1, p, at, :] = lo

    accel(1)

    def scatter(acc, rhs, hits, values):
        parts = ([], [])
        for v in values:
            for side, piece in zip(parts, split(v)):
                side.append(hits * piece)
        o = acc[...]
        for side in parts:
            lhs = side[0] if len(side) == 1 else jnp.concatenate(side, axis=0)
            o = o + lax.dot_general(lhs, rhs, (((1,), (1,)), ((), ())), preferred_element_type=F32)
        acc[...] = o

    acce[...] = jnp.zeros_like(acce)

    @pl.loop(0, wide)
    def _(t):
        scatter(acce, zs[t], rs[t], [line_up(wbuf, t, 4)])

    for c in gm:
        c.wait()
    g = gms[...]
    for d in range(1, nby):
        g = jnp.maximum(g, gmr[d - 1])
    gsx[...] = g
    gall[X] = g

    @pl.loop(1, nbx)
    def _(d):
        sending(gsx, gall, esg, erg, lax.rem(X + d, nbx), d).start()

    @pl.loop(0, tiles)
    def _(t):
        for f, g in enumerate(gather(taba[0, 1], taba[1, 1], zm[t], mrow[t] - cy, cy)):
            snd_l[2 * t, f : f + 1, :] = g[:, :128]
            snd_l[2 * t + 1, f : f + 1, :] = g[:, 128:]

    for c in up:
        c.wait()
    accel(0)
    mine = X // 2

    @pl.loop(0, tiles)
    def _(i):
        t = lax.rem(i + mine, tiles)
        for f, g in enumerate(gather(taba[0, 0], taba[1, 0], zm[t], mrow[t], cy)):
            snd_l[2 * t, f : f + 1, :] = snd_l[2 * t, f : f + 1, :] + g[:, :128]
            snd_l[2 * t + 1, f : f + 1, :] = snd_l[2 * t + 1, f : f + 1, :] + g[:, 128:]
        for k in range(2):
            to = 2 * t + k

            @pl.when(to != X)
            def _():
                sending(snd_l.at[to], rcv_l, esl, erl, to, lax.rem(to - X + nbx, nbx)).start()
    rcv_l[X] = snd_l[X]

    @pl.loop(1, nbx)
    def _(d):
        sending(gsx, gall, esg, erg, lax.rem(X + d, nbx), d).wait_send()
        arriving(gsx, gall, esg, erg, lax.rem(X + nbx - d, nbx)).wait_recv()
    g = lax.fori_loop(1, nbx, lambda d, c: jnp.maximum(c, gall[d]), gall[0])
    g = jnp.max(jnp.max(g, axis=0, keepdims=True), axis=1, keepdims=True)
    dt = 0.25 / jnp.broadcast_to(g, (8, nz))
    dt_row = dt[0:1, 0:128]

    accl[...] = jnp.zeros_like(accl)

    def late_scatter(p):
        @pl.loop(0, wide)
        def _(i):
            t = lax.rem(X // 4 - i + wide, wide)
            if p == 0:
                for k in range(4):
                    frm = 4 * t + k

                    @pl.when(frm != X)
                    def _():
                        arriving(snd_l.at[frm], rcv_l, esl, erl, frm).wait_recv()
            w = line_up(wbuf, t, 4)
            values = []
            for f in range(3):
                moved = [
                    rcv_e[4 * t + k, f : f + 1, :] + dt_row * rcv_l[4 * t + k, f : f + 1, :]
                    for k in range(4)
                ]
                values.append(w * jnp.concatenate(moved, axis=1))
            scatter(accl.at[p], zs[t], rs[t, p * cy : (p + 1) * cy, :], values)

    def move(p):
        @pl.loop(0, cy // 8)
        def _(i):
            b = pl.multiple_of(i * 8, 8)
            at = pl.multiple_of(p * cy + b, 8)
            keep = 1.0 - acce[pl.ds(at, 8), :]
            for f in range(3):
                v = nod[3 + f, p, pl.ds(8 + b, 8), :] + dt * frc[f, p, pl.ds(b, 8), :]
                v = v * keep + accl[p, pl.ds(pl.multiple_of(f * cy + b, 8), 8), :]
                velb[f, p, pl.ds(b, 8), :] = v
                mov[f, p, pl.ds(8 + b, 8), :] = nod[f, p, pl.ds(8 + b, 8), :] + dt * v

    late_scatter(0)
    move(0)
    for c in late[:3]:
        c.start()
    late_scatter(1)
    move(1)
    late[3].start()
    outs = [
        pltpu.make_async_copy(velb, vel_x, osem.at[0]),
        pltpu.make_async_copy(old.at[:, 1, body], old_x, osem.at[1]),
        pltpu.make_async_copy(mov.at[:, 0, body], mov_x.at[:, 0, body], osem.at[2]),
        pltpu.make_async_copy(mov.at[:, 1, body], mov_x.at[:, 1, body], osem.at[3]),
    ]
    for c in outs:
        c.start()

    @pl.loop(1, nbx)
    def _(d):
        to = lax.rem(X + d, nbx)
        sending(snd_l.at[to], rcv_l, esl, erl, to, d).wait_send()

    late[2].wait()
    late[3].wait()

    @pl.loop(0, cy // 8)
    def _(i):
        b = pl.multiple_of(i * 8, 8)
        r = pl.multiple_of(8 + b, 8)
        at = pl.ds(r, 8)
        d, e = finish(mov, 0, r, mas[1, at, :], ene[0, at, :], old[0, 0, at, :], old[1, 0, at, :])
        fin[0, pl.ds(b, 8), :] = d
        fin[1, pl.ds(b, 8), :] = e
    ends = [
        pltpu.make_async_copy(fin, fin_x, osem.at[4]),
        pltpu.make_async_copy(mov.at[:, 1, top], mov_x.at[:, 1, top], osem.at[5]),
    ]
    ends[0].start()
    ends[1].start()
    late[0].wait()
    late[1].wait()
    for c in outs + ends:
        c.wait()


def write_out(
    cy, nz, vel_x, mov_x, fin_x, old_x, mass, ener, vel_o, disp_o, den_o, ene_o,
    velb, mov, fin, old, mas, ene, res, isem, osem,
):
    body = pl.ds(8, cy)
    ins = [
        (mov_x.at[:, 1, pl.ds(8, cy + 8)], mov.at[:, 1, pl.ds(8, cy + 8)]),
        (mov_x.at[:, 2, pl.ds(8, cy + 8)], mov.at[:, 2, pl.ds(8, cy + 8)]),
        (old_x, old),
        (mass.at[1], mas),
        (ener.at[1], ene),
        (mov_x.at[:, 0, body], mov.at[:, 0, body]),
        (vel_x, velb),
        (fin_x, fin),
    ]
    ins = [pltpu.make_async_copy(s, d, isem.at[i]) for i, (s, d) in enumerate(ins)]
    for c in ins:
        c.start()
    for c in ins[:5]:
        c.wait()

    def step(i, _):
        b = pl.multiple_of(i * 8, 8)
        at = pl.ds(b, 8)
        d, e = finish(
            mov, 1, pl.multiple_of(8 + b, 8), mas[at, :], ene[at, :], old[0, at, :], old[1, at, :]
        )
        res[0, at, :] = d
        res[1, at, :] = e
        return 0

    half = cy // 16
    lax.fori_loop(0, half, step, 0)
    for c in ins[5:]:
        c.wait()
    outs = [
        (velb, vel_o),
        (mov.at[:, 0:2, body], disp_o),
        (fin.at[0], den_o.at[0]),
        (fin.at[1], ene_o.at[0]),
        (res.at[0], den_o.at[1]),
        (res.at[1], ene_o.at[1]),
    ]
    outs = [pltpu.make_async_copy(s, d, osem.at[i]) for i, (s, d) in enumerate(outs)]
    for c in outs[:4]:
        c.start()
    lax.fori_loop(half, cy // 8, step, 0)
    for c in outs[4:]:
        c.start()
    for c in outs:
        c.wait()


def solution(mesh):
    nbx, nby = mesh.shape["bx"], mesh.shape["by"]

    def local(displacement, velocity, zone_mass, energy, send_index, recv_index, contact_live):
        _, cx, cy, nz = displacement.shape
        displacement, velocity, zone_mass, energy, send_index, recv_index, contact_live = [
            pltpu.with_memory_space_constraint(x, pltpu.HBM)
            for x in (displacement, velocity, zone_mass, energy, send_index, recv_index, contact_live)
        ]
        rows = cx * cy
        bounds = (0, 48, 88, 112, 128) if cy == 128 else (0, cy // 2, cy)
        chunks = len(bounds) - 1
        tiles, wide = nbx // 2, nbx // 4
        tall = cy + 16
        copies = 12 + 2 * chunks + chunks + nby - 1 + 4
        anywhere = pl.BlockSpec(memory_space=pl.ANY)
        V = pltpu.VMEM
        DMA = pltpu.SemaphoreType.DMA
        scratch = [
            V((6, 3, tall, nz), F32),
            V((3, cy + 8, nz), F32),
            V((cx, cy + 8, nz), F32),
            V((2, cx, cy + 8, nz), F32),
            V((2, cy, nz), F32),
            V((3, cx, cy, nz), F32),
            V((9, cy + 8, nz), F32),
            V((3, cy, nz), F32),
            V((3, cy, nz), F32),
            V((cx, cy, nz), F32),
            V((3, 3, tall, nz), F32),
            V((3, cx, cy, nz), F32),
            V((nbx, 128), jnp.int32),
            V((nbx, 128), jnp.int32),
            V((nbx, 128), jnp.int32),
            V((nbx, 128), F32),
            V((tiles, nz, 256), BF16),
            V((tiles, 1, 256), jnp.int32),
            V((wide, nz, 512), BF16),
            V((wide, 1, 512), jnp.int32),
            V((wide, rows, 512), BF16),
            V((2, 4 * rows, nz), BF16),
            V((2, cx, 3 * cy, nz), BF16),
            V((rows, nz), F32),
            V((cx, 3 * cy, nz), F32),
            V((nbx, 4, 128), F32),
            V((nbx, 4, 128), F32),
            V((nbx, 4, 128), F32),
            V((nbx, 4, 128), F32),
            V((8, nz), F32),
            V((8, 128), F32),
            V((nby - 1, 8, 128), F32),
            V((8, 128), F32),
            V((nbx, 8, 128), F32),
            DMA((7,)),
            DMA((7,)),
            DMA((copies,)),
            DMA((copies,)),
            DMA((nbx,)),
            DMA((nbx,)),
            DMA((nbx,)),
            DMA((nbx,)),
            DMA((nbx,)),
            DMA((nbx,)),
        ]
        flat = zone_mass.shape
        shapes = (displacement.shape, (3, 3, tall, nz), (2, cy, nz), (2, cy, nz))
        vel_x, mov_x, fin_x, old_x = pl.pallas_call(
            functools.partial(kernel, nbx, nby, cx, cy, nz, bounds),
            out_shape=tuple(jax.ShapeDtypeStruct(s, F32) for s in shapes),
            in_specs=[anywhere] * 7,
            out_specs=(anywhere,) * 4,
            scratch_shapes=scratch,
            compiler_params=pltpu.CompilerParams(
                collective_id=0, has_side_effects=True, vmem_limit_bytes=40 * 1024 * 1024
            ),
        )(displacement, velocity, zone_mass, energy, send_index, recv_index, contact_live)
        return pl.pallas_call(
            functools.partial(write_out, cy, nz),
            out_shape=tuple(
                jax.ShapeDtypeStruct(s, F32) for s in (displacement.shape, displacement.shape, flat, flat)
            ),
            in_specs=[anywhere] * 6,
            out_specs=(anywhere,) * 4,
            scratch_shapes=[
                V((3, cx, cy, nz), F32),
                V((3, 3, tall, nz), F32),
                V((2, cy, nz), F32),
                V((2, cy, nz), F32),
                V((cy, nz), F32),
                V((cy, nz), F32),
                V((2, cy, nz), F32),
                DMA((8,)),
                DMA((6,)),
            ],
            compiler_params=pltpu.CompilerParams(vmem_limit_bytes=16 * 1024 * 1024),
        )(vel_x, mov_x, fin_x, old_x, zone_mass, energy)

    field = P(None, "bx", "by", None)
    flat = P("bx", "by", None)
    panel = P("bx", "by", None, None)
    return jax.shard_map(
        local,
        mesh=mesh,
        in_specs=(field, field, flat, flat, panel, panel, panel),
        out_specs=(field, field, flat, flat),
        check_vma=False,
    )
```
